256 devices in a mesh: group: 4 (over y), row: 16 (over x, z_lo), col: 4 (over z_hi, core).
Axes of the slice: x: 4, y: 4, z: 8 (z_hi: 2, z_lo: 4; z = z_hi * 4 + z_lo), core: 2. Of those that a mesh axis runs over, the one named last changes fastest.
Arguments:
- fronts: bfloat16 [8, 12288, 12288], P('group', 'row', 'col'), may hold values from -0.0546875 to 0.0546875
- samples: bfloat16 [256, 8, 12288], P('row', 'group', 'col'), may hold values from -6 to 6
- second_samples: bfloat16 [256, 8, 12288], P('col', 'group', 'row'), may hold values from -6 to 6
- front_sizes: int32 [8], replicated, may hold values from 1536 to 12288, as said below
- parent_ids: int32 [8], replicated, may hold values from 1 to 8, as said below
- block_maps: int32 [8, 16], replicated, may hold values from 0 to 16, as said below
Outputs:
- sampled: bfloat16 [256, 8, 12288], P('col', 'group', 'row')
- projected: bfloat16 [256, 8, 12288], P('row', 'group', 'col')
The draws below stay inside these ranges and needn't reach their ends.
Inputs may be any that keep to these rules, and one draw needn't show every extreme that they name: `front_sizes`: every front has at least 1536 rows and some front has exactly 12288. `parent_ids`: a front's parent has a larger index; 8 marks a root; the last front is a root. `block_maps`: for a front f with a parent p, entry b with b * 768 < front_sizes[f] names a parent block q with q * 768 < front_sizes[p]; all other entries are 16; several child blocks may name one parent block.
All inputs are finite; a program needn't handle non-finite values.
Results may differ from the reference program's by a relative error of at most 0.009.
Values may be sent and summed in bfloat16 or wider, within the bound.
No kernel may reach another device: no remote copies, remote signals or barrier semaphores. Data moves between devices by JAX's collectives and lax.ppermute only.
A program may use at most 64 MiB of HBM per device.

```python
import jax
import jax.numpy as jnp
from jax import lax

M = 12288
S = 256
FRONTS = 8
NB = 16
BLK = 768


def tree_draw(key):
    base = jax.random.fold_in(key, 7)
    key_sizes, key_top, key_parent, key_blocks = jax.random.split(base, 4)
    indices = jnp.arange(FRONTS, dtype=jnp.int32)
    sizes = jax.random.randint(key_sizes, (FRONTS,), M // 8, M + 1, dtype=jnp.int32)
    largest = jax.random.randint(key_top, (), 0, FRONTS, dtype=jnp.int32)
    sizes = jnp.where(indices == largest, M, sizes)
    parents = jax.random.randint(key_parent, (FRONTS,), indices + 1, FRONTS + 1, dtype=jnp.int32)
    valid = (sizes + BLK - 1) // BLK
    parent_valid = valid[jnp.minimum(parents, FRONTS - 1)]
    targets = jax.random.randint(key_blocks, (FRONTS, NB), 0, parent_valid[:, None], dtype=jnp.int32)
    live = (jnp.arange(NB, dtype=jnp.int32)[None, :] < valid[:, None]) & (parents[:, None] < FRONTS)
    maps = jnp.where(live, targets, NB).astype(jnp.int32)
    return (sizes, parents, maps)


def draw_front_sizes(key, part):
    return tree_draw(key)[0]


def draw_parent_ids(key, part):
    return tree_draw(key)[1]


def draw_block_maps(key, part):
    return tree_draw(key)[2]


def block_levels(rng, extent, shards, least, top_value):
    def one(axis_at, shards_of):
        steps = jax.random.uniform(jax.random.fold_in(jax.random.fold_in(rng, 6), axis_at), (shards_of,), jnp.float32, least / len(shards), top_value / len(shards))
        return jnp.repeat(jnp.exp(steps), extent[axis_at] // shards_of).reshape((-1,) + (1,) * (len(extent) - axis_at - 1))

    gain = one(*shards[0])
    for cut in shards[1:]:
        gain = gain * one(*cut)
    return gain


def normal_values(own_key, dims, spread, reach, cuts=(), kind=jnp.bfloat16):
    array = spread * jax.random.normal(own_key, dims, jnp.float32)
    if cuts:
        array = array * block_levels(own_key, dims, cuts, -0.22, 0.18)
    return jnp.clip(array, -reach, reach).astype(kind)


def setup_inputs(seed: int = 0) -> dict:
    streams_of = jax.random.split(jax.random.key(seed), 7)
    fronts = normal_values(streams_of[0], (FRONTS, M, M), M ** -0.5, 0.0546875, ((0, 4), (1, 16), (2, 4)))
    samples = normal_values(streams_of[1], (S, FRONTS, M), 1.0, 6.0, ((0, 16), (1, 4), (2, 4)))
    second_samples = normal_values(streams_of[2], (S, FRONTS, M), 1.0, 6.0, ((0, 4), (1, 4), (2, 16)))
    front_sizes = draw_front_sizes(jax.random.fold_in(streams_of[6], 71), 0)
    parent_ids = draw_parent_ids(jax.random.fold_in(streams_of[6], 71), 0)
    block_maps = draw_block_maps(jax.random.fold_in(streams_of[6], 71), 0)
    return dict(fronts=fronts, samples=samples, second_samples=second_samples, front_sizes=front_sizes, parent_ids=parent_ids, block_maps=block_maps)


def reference(fronts, samples, second_samples, front_sizes, parent_ids, block_maps):
    positions = jnp.arange(M, dtype=jnp.int32)
    first_rows = []
    for front_index in range(FRONTS):
        keep_mask = (positions < front_sizes[front_index]).astype(jnp.float32)
        front_wide = fronts[front_index].astype(jnp.float32)
        chosen = samples[:, front_index, :].astype(jnp.float32) * keep_mask[None, :]
        product = jnp.einsum('sk,mk->sm', chosen, front_wide, precision=lax.Precision.HIGHEST)
        first_rows.append(product * keep_mask[None, :])
    sampled = jnp.stack(first_rows, axis=1).astype(jnp.bfloat16)
    parent_hot = (parent_ids[:, None] == jnp.arange(FRONTS, dtype=jnp.int32)[None, :]).astype(jnp.float32)
    block_hot = (block_maps[:, :, None] == jnp.arange(NB, dtype=jnp.int32)[None, None, :]).astype(jnp.float32)
    routing = jnp.einsum('fp,fbq->fpbq', parent_hot, block_hot)
    blocked = sampled.astype(jnp.float32).reshape(S, FRONTS, NB, BLK)
    extension = jnp.einsum('fpbq,sfbk->spqk', routing, blocked, precision=lax.Precision.HIGHEST)
    extension = extension.reshape(S, FRONTS, M)
    combined = (second_samples.astype(jnp.float32) + extension).astype(jnp.bfloat16)
    second_rows = []
    for front_index in range(FRONTS):
        keep_mask = (positions < front_sizes[front_index]).astype(jnp.float32)
        front_wide = fronts[front_index].astype(jnp.float32)
        chosen = combined[:, front_index, :].astype(jnp.float32) * keep_mask[None, :]
        product = jnp.dot(chosen, front_wide, precision=lax.Precision.HIGHEST)
        second_rows.append(product * keep_mask[None, :])
    projected = jnp.stack(second_rows, axis=1).astype(jnp.bfloat16)
    return sampled, projected
```

```python
import jax
import jax.numpy as jnp
from jax import lax
from jax.sharding import Mesh
from jax.sharding import PartitionSpec as P

DEVICES = ("group", "x", "z", "h", "c")
ROW = ("x", "z")
COL = ("h", "c")
F32 = jnp.float32
BF16 = jnp.bfloat16


def shift(value, axis, by):
    n = lax.axis_size(axis)
    return lax.ppermute(value, axis, [(i, (i + by) % n) for i in range(n)])


def pick(value, index):
    return lax.dynamic_index_in_dim(value, index, 0, keepdims=False)


def rolled(value, start):
    twice = jnp.concatenate([value, value], axis=0)
    return lax.dynamic_slice_in_dim(twice, start, value.shape[0], 0)


def gather_rows(own):
    column = jnp.concatenate([own] + [shift(own, "z", -k) for k in (1, 2, 3)], axis=0)
    half = column.shape[0] // 2
    left = shift(column, "x", 1)
    right = shift(column, "x", -1)
    over_left = shift(left[:half], "x", 1)
    over_right = shift(right[half:], "x", -1)
    return jnp.concatenate([column, over_left, over_right, left, right], axis=0)


def reduce_cols(partial, x, h, c):
    odd = (x - c) & 1
    received = shift(pick(partial, 1 - odd), "c", 1)
    pair = pick(partial, odd).astype(F32) + received.astype(F32)
    kept = h ^ (((x - odd) & 3) >> 1)
    received = shift(pick(pair, 1 - kept).astype(BF16), "h", 1)
    return pick(pair, kept) + received.astype(F32)


def scatter_rows(product):
    block = product.shape[0] // 4
    half = block // 2
    to_right = shift(product[block + half : 2 * block + half], "x", 1)
    to_left = shift(product[2 * block + half : 3 * block + half], "x", -1)
    over_right = product[block : block + half].astype(F32) + to_right[half:].astype(F32)
    over_left = product[3 * block + half :].astype(F32) + to_left[:half].astype(F32)
    over_right = shift(over_right.astype(BF16), "x", 1)
    over_left = shift(over_left.astype(BF16), "x", -1)
    top = product[:half].astype(F32) + to_left[half:].astype(F32) + over_right.astype(F32)
    low = product[half:block].astype(F32) + to_right[:half].astype(F32) + over_left.astype(F32)
    own = jnp.concatenate([top, low], axis=0)
    rows = block // 4
    total = own[:rows]
    for k in (1, 2, 3):
        piece = own[k * rows : (k + 1) * rows].astype(BF16)
        total = total + shift(piece, "z", k).astype(F32)
    return total


def shards(fronts, samples, second_samples, front_sizes, parent_ids, block_maps):
    local, tile_rows, tile_cols = fronts.shape
    own_rows = samples.shape[0]
    slab = second_samples.shape[0]
    group, x, z, h, c = (lax.axis_index(axis) for axis in DEVICES)
    row = lax.axis_index(ROW)
    col = lax.axis_index(COL)
    count = parent_ids.shape[0]
    blocks = block_maps.shape[1]

    row_keep, col_keep = [], []
    for f in range(local):
        size = lax.dynamic_index_in_dim(front_sizes, group * local + f, 0, keepdims=False)
        row_keep.append((row * tile_rows + jnp.arange(tile_rows, dtype=jnp.int32) < size)[None, :])
        col_keep.append((col * tile_cols + jnp.arange(tile_cols, dtype=jnp.int32) < size)[None, :])
    zero = jnp.zeros((), BF16)

    slabs = []
    for f in range(local):
        own = jnp.where(col_keep[f], samples[:, f, :], zero)
        gathered = gather_rows(own)
        partial = jnp.einsum("sk,mk->sm", gathered, fronts[f], preferred_element_type=F32)
        partial = jnp.where(row_keep[f], partial, 0.0).astype(BF16)
        total = reduce_cols(partial.reshape(2, 2, slab, tile_rows), x, h, c)
        total = total.astype(BF16).reshape(-1, own_rows, tile_rows)
        slabs.append(rolled(total, (4 - z) & 3).reshape(slab, tile_rows))
    sampled = jnp.stack(slabs, axis=1)

    spread = ("group",) + ROW
    flat = jnp.concatenate(slabs, axis=1)
    arrived = lax.all_to_all(flat, spread, split_axis=0, concat_axis=0, tiled=True)
    arrived = arrived.reshape(-1, tile_rows)
    front_of = jnp.arange(count, dtype=jnp.int32)
    parent_match = parent_ids[:, None] == front_of[None, :]
    block_match = block_maps[:, :, None] == jnp.arange(blocks, dtype=jnp.int32)[None, None, :]
    weight = parent_match[:, None, :, None] & block_match[:, :, None, :]
    groups = count // local
    weight = weight.reshape(groups, local, blocks, groups, local, blocks)
    weight = weight.transpose(3, 5, 4, 0, 2, 1).reshape(count * blocks, count * blocks).astype(BF16)
    extension = jnp.einsum("ij,jk->ik", weight, arrived, preferred_element_type=F32).astype(BF16)
    extension = extension.reshape(slab, local * tile_rows)
    extension = lax.all_to_all(extension, spread, split_axis=0, concat_axis=0, tiled=True)
    extension = extension.reshape(slab, local, tile_rows)

    outs = []
    for f in range(local):
        combined = (second_samples[:, f, :].astype(F32) + extension[:, f, :].astype(F32)).astype(BF16)
        combined = jnp.where(row_keep[f], combined, zero).reshape(-1, own_rows, tile_rows)
        combined = rolled(combined, z).reshape(slab, tile_rows)
        pair = jnp.stack([combined, shift(combined, "h", 1)])
        quad = jnp.stack([pair, shift(pair, "c", 1)], axis=1).reshape(4, slab, tile_rows)
        ordered = jnp.concatenate([pick(quad, ((x + k) & 3) ^ col) for k in range(4)], axis=0)
        product = jnp.einsum("sm,mk->sk", ordered, fronts[f], preferred_element_type=F32)
        total = scatter_rows(product.astype(BF16))
        outs.append(jnp.where(col_keep[f], total, 0.0).astype(BF16))
    return sampled, jnp.stack(outs, axis=1)


def solution(mesh):
    torus = Mesh(mesh.devices.reshape(mesh.shape["group"], 4, 4, 2, 2), DEVICES)
    in_specs = (P("group", ROW, COL), P(ROW, "group", COL), P(COL, "group", ROW), P(), P(), P())
    out_specs = (P(COL, "group", ROW), P(ROW, "group", COL))
    return jax.shard_map(
        shards, mesh=torus, in_specs=in_specs, out_specs=out_specs, check_vma=False
    )
```

```python
import jax
import jax.numpy as jnp
from jax import lax
from jax.experimental import pallas as pl
from jax.experimental.pallas import tpu as pltpu
from jax.sharding import Mesh
from jax.sharding import PartitionSpec as P

DEVICES = ("group", "x", "z", "h", "c")
ROW = ("x", "z")
COL = ("h", "c")
F32 = jnp.float32
BF16 = jnp.bfloat16


def shift(value, axis, by):
    n = lax.axis_size(axis)
    return lax.ppermute(value, axis, [(i, (i + by) % n) for i in range(n)])


def pick(value, index):
    return lax.dynamic_index_in_dim(value, index, 0, keepdims=False)


def rolled(value, start):
    twice = jnp.concatenate([value, value], axis=0)
    return lax.dynamic_slice_in_dim(twice, start, value.shape[0], 0)


def ring_copies(mine):
    half = mine.shape[0] // 2
    left = shift(mine, "x", 1)
    right = shift(mine, "x", -1)
    over_left = shift(left[:half], "x", 1)
    over_right = shift(right[half:], "x", -1)
    return jnp.concatenate([mine, over_left, over_right, left, right], axis=0)


def gather_rows(samples):
    columns = []
    for f in range(samples.shape[1]):
        mine = samples[:, f, :]
        columns.append(jnp.concatenate([mine] + [shift(mine, "z", -k) for k in (1, 2, 3)], axis=0))
    return [ring_copies(column) for column in columns]


def mask_kernel(sizes_ref, origin_ref, fronts_ref, out_ref):
    tile = fronts_ref[...]
    size = sizes_ref[pl.program_id(0)]
    rows = origin_ref[0] + pl.program_id(1) * tile.shape[1] + lax.broadcasted_iota(jnp.int32, tile.shape, 1)
    cols = origin_ref[1] + lax.broadcasted_iota(jnp.int32, tile.shape, 2)
    out_ref[...] = jnp.where(jnp.maximum(rows, cols) < size, tile, jnp.zeros((), tile.dtype))


def masked_fronts(fronts, sizes, origin):
    local, rows, cols = fronts.shape
    step = 64
    spec = pl.BlockSpec((1, step, cols), lambda f, i: (f, i, 0))
    scalars = pl.BlockSpec(memory_space=pltpu.SMEM)
    return pl.pallas_call(
        mask_kernel,
        grid=(local, rows // step),
        in_specs=[scalars, scalars, spec],
        out_specs=spec,
        out_shape=jax.ShapeDtypeStruct(fronts.shape, fronts.dtype),
        compiler_params=pltpu.CompilerParams(vmem_limit_bytes=4 << 20),
    )(sizes, origin, fronts)


def reduce_cols(partial, x, h, c):
    odd = (x - c) & 1
    received = shift(pick(partial, 1 - odd), "c", 1)
    pair = pick(partial, odd).astype(F32) + received.astype(F32)
    kept = h ^ (((x - odd) & 3) >> 1)
    received = shift(pick(pair, 1 - kept).astype(BF16), "h", 1)
    return pick(pair, kept) + received.astype(F32)


def scatter_rows(product):
    block = product.shape[0] // 4
    half = block // 2
    to_right = shift(product[block + half : 2 * block + half], "x", 1)
    to_left = shift(product[2 * block + half : 3 * block + half], "x", -1)
    over_right = product[block : block + half].astype(F32) + to_right[half:].astype(F32)
    over_left = product[3 * block + half :].astype(F32) + to_left[:half].astype(F32)
    over_right = shift(over_right.astype(BF16), "x", 1)
    over_left = shift(over_left.astype(BF16), "x", -1)
    top = product[:half].astype(F32) + to_left[half:].astype(F32) + over_right.astype(F32)
    low = product[half:block].astype(F32) + to_right[:half].astype(F32) + over_left.astype(F32)
    own = jnp.concatenate([top, low], axis=0)
    rows = block // 4
    total = own[:rows]
    for k in (1, 2, 3):
        piece = own[k * rows : (k + 1) * rows].astype(BF16)
        total = total + shift(piece, "z", k).astype(F32)
    return total


def shards(fronts, samples, second_samples, front_sizes, parent_ids, block_maps):
    local, tile_rows, tile_cols = fronts.shape
    own_rows = samples.shape[0]
    slab = second_samples.shape[0]
    group, x, z, h, c = (lax.axis_index(axis) for axis in DEVICES)
    row = lax.axis_index(ROW)
    col = lax.axis_index(COL)
    count = parent_ids.shape[0]
    blocks = block_maps.shape[1]

    sizes = lax.dynamic_slice_in_dim(front_sizes, group * local, local, 0)
    masked = masked_fronts(fronts, sizes, jnp.stack([row * tile_rows, col * tile_cols]))

    slabs = []
    for f, gathered in enumerate(gather_rows(samples)):
        partial = jnp.einsum("sk,mk->sm", gathered, masked[f], preferred_element_type=F32)
        total = reduce_cols(partial.astype(BF16).reshape(2, 2, slab, tile_rows), x, h, c)
        total = total.astype(BF16).reshape(-1, own_rows, tile_rows)
        slabs.append(rolled(total, (4 - z) & 3).reshape(slab, tile_rows))
    sampled = jnp.stack(slabs, axis=1)

    spread = ("group",) + ROW
    arrived = lax.all_to_all(sampled, spread, split_axis=0, concat_axis=0, tiled=True)
    front_of = jnp.arange(count, dtype=jnp.int32)
    parent_match = parent_ids[:, None] == front_of[None, :]
    block_match = block_maps[:, :, None] == jnp.arange(blocks, dtype=jnp.int32)[None, None, :]
    weight = parent_match[:, None, :, None] & block_match[:, :, None, :]
    groups = count // local
    weight = weight.reshape(groups, local, blocks, groups, local, blocks)
    weight = weight.transpose(3, 5, 4, 0, 2, 1).reshape(count * blocks, count * blocks).astype(BF16)
    arrived = arrived.reshape(-1, tile_rows)
    extension = jnp.einsum("ij,jk->ik", weight, arrived, preferred_element_type=F32).astype(BF16)
    extension = extension.reshape(slab, local, tile_rows)
    extension = lax.all_to_all(extension, spread, split_axis=0, concat_axis=0, tiled=True)
    combined = (second_samples.astype(F32) + extension.astype(F32)).astype(BF16)

    mine = []
    for f in range(local):
        blocked = combined[:, f, :].reshape(-1, own_rows, tile_rows)
        mine.append(rolled(blocked, z).reshape(slab, tile_rows))
    everyone = lax.all_gather(jnp.concatenate(mine, axis=1), COL, axis=0, tiled=True)
    outs = []
    for f in range(local):
        ordered = everyone[:, f * tile_rows : (f + 1) * tile_rows].reshape(-1, slab, tile_rows)
        ordered = rolled(ordered, x).reshape(-1, tile_rows)
        product = jnp.einsum("sm,mk->sk", ordered, masked[f], preferred_element_type=F32)
        outs.append(scatter_rows(product.astype(BF16)).astype(BF16))
    return sampled, jnp.stack(outs, axis=1)


def solution(mesh):
    torus = Mesh(mesh.devices.reshape(mesh.shape["group"], 4, 4, 2, 2), DEVICES)
    in_specs = (P("group", ROW, COL), P(ROW, "group", COL), P(COL, "group", ROW), P(), P(), P())
    out_specs = (P(COL, "group", ROW), P(ROW, "group", COL))
    return jax.shard_map(
        shards, mesh=torus, in_specs=in_specs, out_specs=out_specs, check_vma=False
    )
```

```python
import jax
import jax.numpy as jnp
from jax import lax
from jax.experimental import pallas as pl
from jax.experimental.pallas import tpu as pltpu
from jax.sharding import Mesh
from jax.sharding import PartitionSpec as P

DEVICES = ("group", "x", "z", "h", "c")
ROW = ("x", "z")
COL = ("h", "c")
F32 = jnp.float32
BF16 = jnp.bfloat16


def shift(value, axis, by):
    n = lax.axis_size(axis)
    return lax.ppermute(value, axis, [(i, (i + by) % n) for i in range(n)])


def pick(value, index):
    return lax.dynamic_index_in_dim(value, index, 0, keepdims=False)


def rolled(value, starts):
    sizes = value.shape
    for axis in range(len(starts)):
        value = jnp.concatenate([value, value], axis=axis)
    starts = tuple(starts) + (0,) * (len(sizes) - len(starts))
    return lax.dynamic_slice(value, starts, sizes)


def gather_rows(columns):
    left = shift(columns, "x", 1)
    right = shift(columns, "x", -1)
    over = (shift(left[0], "x", 1), shift(right[1], "x", -1))
    return [jnp.concatenate([columns[f], over[f], left[f], right[f]], axis=0) for f in range(2)]


def mask_kernel(sizes_ref, origin_ref, fronts_ref, out_ref):
    tile = fronts_ref[...]
    size = sizes_ref[pl.program_id(0)]
    rows = origin_ref[0] + pl.program_id(1) * tile.shape[1] + lax.broadcasted_iota(jnp.int32, tile.shape, 1)
    cols = origin_ref[1] + lax.broadcasted_iota(jnp.int32, tile.shape, 2)
    out_ref[...] = jnp.where(jnp.maximum(rows, cols) < size, tile, jnp.zeros((), tile.dtype))


def masked_fronts(fronts, sizes, origin):
    local, rows, cols = fronts.shape
    step = 64
    spec = pl.BlockSpec((1, step, cols), lambda f, i: (f, i, 0))
    scalars = pl.BlockSpec(memory_space=pltpu.SMEM)
    return pl.pallas_call(
        mask_kernel,
        grid=(local, rows // step),
        in_specs=[scalars, scalars, spec],
        out_specs=spec,
        out_shape=jax.ShapeDtypeStruct(fronts.shape, fronts.dtype),
        compiler_params=pltpu.CompilerParams(vmem_limit_bytes=4 << 20),
    )(sizes, origin, fronts)


def reduce_core(partial, x, c):
    odd = (x - c) & 1
    received = shift(pick(partial, 1 - odd), "c", 1)
    total = pick(partial, odd).astype(F32) + received.astype(F32)
    return rolled(total, (((x - odd) & 3) >> 1,))


def first_pieces(product):
    block = product.shape[0] // 4
    half = block // 2
    to_right = product[block + half : 2 * block + half]
    to_left = jnp.concatenate([product[block : block + half], product[3 * block + half :]], axis=0)
    return to_right, to_left


def scatter_rows(products, pieces):
    block = products[0].shape[0] // 4
    half = block // 2
    rows = block // 4
    near = []
    for to_right, to_left in pieces:
        near.append(lax.optimization_barrier((shift(to_right, "x", 1), shift(to_left, "x", -1))))
    far = []
    for product, (from_left, from_right) in zip(products, near):
        over_right = product[2 * block + half : 3 * block].astype(F32) + from_left[:half].astype(F32)
        over_left = product[3 * block : 3 * block + half].astype(F32) + from_right[:half].astype(F32)
        over_right = shift(over_right.astype(BF16), "x", 1)
        over_left = shift(over_left.astype(BF16), "x", -1)
        far.append(lax.optimization_barrier((over_right, over_left)))
    totals = []
    for product, (from_left, from_right), (over_right, over_left) in zip(products, near, far):
        top = product[:half].astype(F32) + from_left[half:].astype(F32) + over_left.astype(F32)
        low = product[half:block].astype(F32) + from_right[half:].astype(F32) + over_right.astype(F32)
        own = jnp.concatenate([top, low], axis=0)
        total = own[:rows]
        for k in (1, 2, 3):
            piece = own[k * rows : (k + 1) * rows].astype(BF16)
            total = total + shift(piece, "z", k).astype(F32)
        totals.append(total)
    return totals


def route_weight(parent_ids, block_maps, local):
    count, blocks = block_maps.shape
    order = (count // local, local, blocks)
    parent = jnp.broadcast_to(parent_ids[:, None], block_maps.shape).reshape(order)
    parent = parent.transpose(0, 2, 1).reshape(1, -1)
    block = block_maps.reshape(order).transpose(0, 2, 1).reshape(1, -1)
    index = lax.broadcasted_iota(jnp.int32, (count * blocks, 1), 0)
    to_parent = index // (blocks * local) * local + index % local
    to_block = index // local % blocks
    return ((parent == to_parent) & (block == to_block)).astype(BF16)


def shards(fronts, samples, second_samples, front_sizes, parent_ids, block_maps):
    local, tile_rows, tile_cols = fronts.shape
    own_rows = samples.shape[0]
    slab = second_samples.shape[0]
    group, x, z, h, c = (lax.axis_index(axis) for axis in DEVICES)
    row = lax.axis_index(ROW)
    col = lax.axis_index(COL)

    mine = jnp.stack([samples[:, f, :] for f in range(local)])
    columns = lax.all_gather(mine, "z", axis=1, tiled=True)
    gathered = gather_rows(columns)
    sizes = lax.dynamic_slice_in_dim(front_sizes, group * local, local, 0)
    second, sizes, columns = lax.optimization_barrier((second_samples, sizes, columns))
    second_of_pair = shift(second, "h", 1)
    masked = masked_fronts(fronts, sizes, jnp.stack([row * tile_rows, col * tile_cols]))
    weight = route_weight(parent_ids, block_maps, local)
    gathered[0], second_of_pair, weight = lax.optimization_barrier((gathered[0], second_of_pair, weight))
    second = rolled(jnp.stack([second, second_of_pair]), (h,))

    halves = []
    for f in range(local):
        partial = jnp.einsum("sk,mk->sm", gathered[f], masked[f], preferred_element_type=F32)
        halves.append(reduce_core(partial.astype(BF16).reshape(2, 2, slab, tile_rows), x, c))

    spread = ("h", "group") + ROW
    outgoing = jnp.stack([half.astype(BF16).reshape(2 * slab, tile_rows) for half in halves], axis=1)
    arrived = lax.all_to_all(outgoing, spread, split_axis=0, concat_axis=0, tiled=True)
    arrived = arrived[:slab].astype(F32) + arrived[slab:].astype(F32)
    arrived = arrived.astype(BF16).reshape(-1, tile_rows)
    extension = jnp.einsum("ij,jk->ik", weight, arrived, preferred_element_type=F32).astype(BF16)
    extension = extension.reshape(slab, local, tile_rows)
    extension = jnp.concatenate([extension, extension], axis=0)
    extension = lax.all_to_all(extension, spread, split_axis=0, concat_axis=0, tiled=True)
    combined = second.reshape(extension.shape).astype(F32) + extension.astype(F32)
    combined = combined.astype(BF16)

    nearer = ((x + ((c - x) & 1)) & 3) >> 1
    ordered = []
    for f in range(local):
        mine = combined[:, f, :].reshape(2, -1, own_rows, tile_rows)
        ordered.append(rolled(mine, (nearer, z)).reshape(2 * slab, tile_rows))
    everyone = lax.all_gather(jnp.stack(ordered), "c", axis=0)
    ordered = [rolled(everyone[:, f], (x & 1,)).reshape(4 * slab, tile_rows) for f in range(local)]
    products, pieces = [], []
    for f in range(local):
        if f > 0:
            ordered[f], pieces[0] = lax.optimization_barrier((ordered[f], pieces[0]))
        product = jnp.einsum("sm,mk->sk", ordered[f], masked[f], preferred_element_type=F32)
        products.append(product.astype(BF16))
        pieces.append(first_pieces(products[f]))

    away = jnp.stack([pick(half, 1 - h).astype(BF16) for half in halves])
    away, products[-1] = lax.optimization_barrier((away, products[-1]))
    received = shift(away, "h", 1)
    totals = scatter_rows(products, pieces)
    received, totals[0] = lax.optimization_barrier((received, totals[0]))
    slabs = [pick(half, h) + received[f].astype(F32) for f, half in enumerate(halves)]
    sampled = jnp.stack([total.astype(BF16) for total in slabs], axis=1)

    outs = [total.astype(BF16) for total in totals]
    return sampled, jnp.stack(outs, axis=1)


def solution(mesh):
    torus = Mesh(mesh.devices.reshape(mesh.shape["group"], 4, 4, 2, 2), DEVICES)
    in_specs = (P("group", ROW, COL), P(ROW, "group", COL), P(COL, "group", ROW), P(), P(), P())
    out_specs = (P(COL, "group", ROW), P(ROW, "group", COL))
    return jax.shard_map(
        shards, mesh=torus, in_specs=in_specs, out_specs=out_specs, check_vma=False
    )
```

```python
import jax
import jax.numpy as jnp
from jax import lax
from jax.experimental import pallas as pl
from jax.experimental.pallas import tpu as pltpu
from jax.sharding import Mesh
from jax.sharding import PartitionSpec as P

DEVICES = ("group", "x", "z", "h", "c")
ROW = ("x", "z")
COL = ("h", "c")
F32 = jnp.float32
BF16 = jnp.bfloat16


def shift(value, axis, by):
    n = lax.axis_size(axis)
    return lax.ppermute(value, axis, [(i, (i + by) % n) for i in range(n)])


def pick(value, index):
    return lax.dynamic_index_in_dim(value, index, 0, keepdims=False)


def rolled(value, starts):
    sizes = value.shape
    for axis in range(len(starts)):
        value = jnp.concatenate([value, value], axis=axis)
    starts = tuple(starts) + (0,) * (len(sizes) - len(starts))
    return lax.dynamic_slice(value, starts, sizes)


def gather_rows(columns):
    left = shift(columns, "x", 1)
    right = shift(columns, "x", -1)
    over = (shift(left[0], "x", 1), shift(right[1], "x", -1))
    return [jnp.concatenate([columns[f], over[f], left[f], right[f]], axis=0) for f in range(2)]


def mask_kernel(sizes_ref, origin_ref, fronts_ref, out_ref):
    tile = fronts_ref[...]
    size = sizes_ref[pl.program_id(0)]
    rows = origin_ref[0] + pl.program_id(1) * tile.shape[1] + lax.broadcasted_iota(jnp.int32, tile.shape, 1)
    cols = origin_ref[1] + lax.broadcasted_iota(jnp.int32, tile.shape, 2)
    out_ref[...] = jnp.where(jnp.maximum(rows, cols) < size, tile, jnp.zeros((), tile.dtype))


def masked_fronts(fronts, sizes, origin):
    local, rows, cols = fronts.shape
    step = 64
    spec = pl.BlockSpec((1, step, cols), lambda f, i: (f, i, 0))
    scalars = pl.BlockSpec(memory_space=pltpu.SMEM)
    return pl.pallas_call(
        mask_kernel,
        grid=(local, rows // step),
        in_specs=[scalars, scalars, spec],
        out_specs=spec,
        out_shape=jax.ShapeDtypeStruct(fronts.shape, fronts.dtype),
        compiler_params=pltpu.CompilerParams(vmem_limit_bytes=4 << 20),
    )(sizes, origin, fronts)


def reduce_core(partial, x, c):
    odd = (x - c) & 1
    received = shift(pick(partial, 1 - odd), "c", 1)
    total = pick(partial, odd).astype(F32) + received.astype(F32)
    return rolled(total, (((x - odd) & 3) >> 1,))


def first_pieces(product):
    block = product.shape[0] // 4
    half = block // 2
    to_right = product[block + half : 2 * block + half]
    to_left = jnp.concatenate([product[block : block + half], product[3 * block + half :]], axis=0)
    return to_right, to_left


def first_step(pieces):
    to_right, to_left = pieces
    return lax.optimization_barrier((shift(to_right, "x", 1), shift(to_left, "x", -1)))


def second_step(product, near):
    block = product.shape[0] // 4
    half = block // 2
    from_left, from_right = near
    over_right = product[2 * block + half : 3 * block].astype(F32) + from_left[:half].astype(F32)
    over_left = product[3 * block : 3 * block + half].astype(F32) + from_right[:half].astype(F32)
    over_right = shift(over_right.astype(BF16), "x", 1)
    over_left = shift(over_left.astype(BF16), "x", -1)
    return lax.optimization_barrier((over_right, over_left))


def last_step(product, near, far):
    block = product.shape[0] // 4
    half = block // 2
    rows = block // 4
    (from_left, from_right), (over_right, over_left) = near, far
    top = product[:half].astype(F32) + from_left[half:].astype(F32) + over_left.astype(F32)
    low = product[half:block].astype(F32) + from_right[half:].astype(F32) + over_right.astype(F32)
    own = jnp.concatenate([top, low], axis=0)
    total = own[:rows]
    for k in (1, 2, 3):
        piece = own[k * rows : (k + 1) * rows].astype(BF16)
        total = total + shift(piece, "z", k).astype(F32)
    return total


def route_weight(parent_ids, block_maps, local):
    count, blocks = block_maps.shape
    order = (count // local, local, blocks)
    parent = jnp.broadcast_to(parent_ids[:, None], block_maps.shape).reshape(order)
    parent = parent.transpose(0, 2, 1).reshape(1, -1)
    block = block_maps.reshape(order).transpose(0, 2, 1).reshape(1, -1)
    index = lax.broadcasted_iota(jnp.int32, (count * blocks, 1), 0)
    to_parent = index // (blocks * local) * local + index % local
    to_block = index // local % blocks
    return ((parent == to_parent) & (block == to_block)).astype(BF16)


def shards(fronts, samples, second_samples, front_sizes, parent_ids, block_maps):
    local, tile_rows, tile_cols = fronts.shape
    own_rows = samples.shape[0]
    slab = second_samples.shape[0]
    group, x, z, h, c = (lax.axis_index(axis) for axis in DEVICES)
    row = lax.axis_index(ROW)
    col = lax.axis_index(COL)

    mine = jnp.stack([samples[:, f, :] for f in range(local)])
    columns = lax.all_gather(mine, "z", axis=1, tiled=True)
    gathered = gather_rows(columns)
    sizes = lax.dynamic_slice_in_dim(front_sizes, group * local, local, 0)
    second, sizes, columns = lax.optimization_barrier((second_samples, sizes, columns))
    second_of_pair = shift(second, "h", 1)
    masked = masked_fronts(fronts, sizes, jnp.stack([row * tile_rows, col * tile_cols]))
    weight = route_weight(parent_ids, block_maps, local)
    gathered[0], second_of_pair, weight = lax.optimization_barrier((gathered[0], second_of_pair, weight))
    second = rolled(jnp.stack([second, second_of_pair]), (h,))

    halves = []
    for f in range(local):
        partial = jnp.einsum("sk,mk->sm", gathered[f], masked[f], preferred_element_type=F32)
        halves.append(reduce_core(partial.astype(BF16).reshape(2, 2, slab, tile_rows), x, c))

    spread = ("h", "group") + ROW
    outgoing = jnp.stack([half.astype(BF16).reshape(2 * slab, tile_rows) for half in halves], axis=1)
    arrived = lax.all_to_all(outgoing, spread, split_axis=0, concat_axis=0, tiled=True)
    arrived = arrived[:slab].astype(F32) + arrived[slab:].astype(F32)
    arrived = arrived.astype(BF16).reshape(-1, tile_rows)
    extension = jnp.einsum("ij,jk->ik", weight, arrived, preferred_element_type=F32).astype(BF16)
    extension = extension.reshape(slab, local, tile_rows)
    extension = jnp.concatenate([extension, extension], axis=0)
    extension = lax.all_to_all(extension, spread, split_axis=0, concat_axis=0, tiled=True)
    combined = second.reshape(extension.shape).astype(F32) + extension.astype(F32)
    combined = combined.astype(BF16)

    nearer = ((x + ((c - x) & 1)) & 3) >> 1
    ordered = []
    for f in range(local):
        mine = combined[:, f, :].reshape(2, -1, own_rows, tile_rows)
        ordered.append(rolled(mine, (nearer, z)).reshape(2 * slab, tile_rows))
    everyone = lax.all_gather(jnp.stack(ordered), "c", axis=0)
    ordered = [rolled(everyone[:, f], (x & 1,)).reshape(4 * slab, tile_rows) for f in range(local)]

    def multiplied(f):
        product = jnp.einsum("sm,mk->sk", ordered[f], masked[f], preferred_element_type=F32)
        return product.astype(BF16)

    product_0 = multiplied(0)
    near_0 = first_step(first_pieces(product_0))
    product_1 = multiplied(1)
    pieces_1 = first_pieces(product_1)
    near_0, product_1, pieces_1 = lax.optimization_barrier((near_0, product_1, pieces_1))
    far_0 = second_step(product_0, near_0)
    near_1 = first_step(pieces_1)
    away = jnp.stack([pick(half, 1 - h).astype(BF16) for half in halves])
    away, far_0 = lax.optimization_barrier((away, far_0))
    received = shift(away, "h", 1)
    total_0 = last_step(product_0, near_0, far_0)
    far_1 = second_step(product_1, near_1)
    received, far_1 = lax.optimization_barrier((received, far_1))
    slabs = [pick(half, h) + received[f].astype(F32) for f, half in enumerate(halves)]
    sampled = jnp.stack([total.astype(BF16) for total in slabs], axis=1)
    total_1 = last_step(product_1, near_1, far_1)
    outs = [total_0.astype(BF16), total_1.astype(BF16)]
    return sampled, jnp.stack(outs, axis=1)


def solution(mesh):
    torus = Mesh(mesh.devices.reshape(mesh.shape["group"], 4, 4, 2, 2), DEVICES)
    in_specs = (P("group", ROW, COL), P(ROW, "group", COL), P(COL, "group", ROW), P(), P(), P())
    out_specs = (P(COL, "group", ROW), P(ROW, "group", COL))
    return jax.shard_map(
        shards, mesh=torus, in_specs=in_specs, out_specs=out_specs, check_vma=False
    )
```

```python
import jax
import jax.numpy as jnp
from jax import lax
from jax.experimental import pallas as pl
from jax.experimental.pallas import tpu as pltpu
from jax.sharding import Mesh
from jax.sharding import PartitionSpec as P

DEVICES = ("group", "x", "z", "h", "c")
ROW = ("x", "z")
COL = ("h", "c")
F32 = jnp.float32
BF16 = jnp.bfloat16


def shift(value, axis, by):
    n = lax.axis_size(axis)
    return lax.ppermute(value, axis, [(i, (i + by) % n) for i in range(n)])


def pick(value, index):
    return lax.dynamic_index_in_dim(value, index, 0, keepdims=False)


def rolled(value, starts):
    sizes = value.shape
    for axis in range(len(starts)):
        value = jnp.concatenate([value, value], axis=axis)
    starts = tuple(starts) + (0,) * (len(sizes) - len(starts))
    return lax.dynamic_slice(value, starts, sizes)


def gather_rows(columns):
    left = shift(columns, "x", 1)
    right = shift(columns, "x", -1)
    over = (shift(left[0], "x", 1), shift(right[1], "x", -1))
    return [jnp.concatenate([columns[f], over[f], left[f], right[f]], axis=0) for f in range(2)]


def mask_kernel(sizes_ref, origin_ref, fronts_ref, out_ref):
    tile = fronts_ref[...]
    size = sizes_ref[pl.program_id(0)]
    rows = origin_ref[0] + pl.program_id(1) * tile.shape[1] + lax.broadcasted_iota(jnp.int32, tile.shape, 1)
    cols = origin_ref[1] + lax.broadcasted_iota(jnp.int32, tile.shape, 2)
    out_ref[...] = jnp.where(jnp.maximum(rows, cols) < size, tile, jnp.zeros((), tile.dtype))


def masked_fronts(fronts, sizes, origin):
    local, rows, cols = fronts.shape
    step = 64
    spec = pl.BlockSpec((1, step, cols), lambda f, i: (f, i, 0))
    scalars = pl.BlockSpec(memory_space=pltpu.SMEM)
    return pl.pallas_call(
        mask_kernel,
        grid=(local, rows // step),
        in_specs=[scalars, scalars, spec],
        out_specs=spec,
        out_shape=jax.ShapeDtypeStruct(fronts.shape, fronts.dtype),
        compiler_params=pltpu.CompilerParams(vmem_limit_bytes=4 << 20),
    )(sizes, origin, fronts)


def reduce_core(partial, x, c):
    odd = (x - c) & 1
    received = shift(pick(partial, 1 - odd), "c", 1)
    total = pick(partial, odd).astype(F32) + received.astype(F32)
    return rolled(total, (((x - odd) & 3) >> 1,))


def first_pieces(product):
    block = product.shape[0] // 4
    half = block // 2
    to_right = product[block + half : 2 * block + half]
    to_left = jnp.concatenate([product[block : block + half], product[3 * block + half :]], axis=0)
    return to_right, to_left


def first_step(pieces):
    to_right, to_left = pieces
    return lax.optimization_barrier((shift(to_right, "x", 1), shift(to_left, "x", -1)))


def second_step(product, near):
    block = product.shape[0] // 4
    half = block // 2
    from_left, from_right = near
    over_right = product[2 * block + half : 3 * block].astype(F32) + from_left[:half].astype(F32)
    over_left = product[3 * block : 3 * block + half].astype(F32) + from_right[:half].astype(F32)
    over_right = shift(over_right.astype(BF16), "x", 1)
    over_left = shift(over_left.astype(BF16), "x", -1)
    return lax.optimization_barrier((over_right, over_left))


def last_step(product, near, far):
    block = product.shape[0] // 4
    half = block // 2
    rows = block // 4
    (from_left, from_right), (over_right, over_left) = near, far
    top = product[:half].astype(F32) + from_left[half:].astype(F32) + over_left.astype(F32)
    low = product[half:block].astype(F32) + from_right[half:].astype(F32) + over_right.astype(F32)
    own = jnp.concatenate([top, low], axis=0)
    total = own[:rows]
    for k in (1, 2, 3):
        piece = own[k * rows : (k + 1) * rows].astype(BF16)
        total = total + shift(piece, "z", k).astype(F32)
    return total


def route_weight(parent_ids, block_maps, local):
    count, blocks = block_maps.shape
    order = (count // local, local, blocks)
    parent = jnp.broadcast_to(parent_ids[:, None], block_maps.shape).reshape(order)
    parent = parent.transpose(0, 2, 1).reshape(1, -1)
    block = block_maps.reshape(order).transpose(0, 2, 1).reshape(1, -1)
    index = lax.broadcasted_iota(jnp.int32, (count * blocks, 1), 0)
    to_parent = index // (blocks * local) * local + index % local
    to_block = index // local % blocks
    return ((parent == to_parent) & (block == to_block)).astype(BF16)


def shards(fronts, samples, second_samples, front_sizes, parent_ids, block_maps):
    local, tile_rows, tile_cols = fronts.shape
    own_rows = samples.shape[0]
    slab = second_samples.shape[0]
    group, x, z, h, c = (lax.axis_index(axis) for axis in DEVICES)
    row = lax.axis_index(ROW)
    col = lax.axis_index(COL)

    mine = jnp.stack([samples[:, f, :] for f in range(local)])
    columns = lax.all_gather(mine, "z", axis=1, tiled=True)
    gathered = gather_rows(columns)
    sizes = lax.dynamic_slice_in_dim(front_sizes, group * local, local, 0)
    second, sizes, columns = lax.optimization_barrier((second_samples, sizes, columns))
    second_of_pair = shift(second, "h", 1)
    masked = masked_fronts(fronts, sizes, jnp.stack([row * tile_rows, col * tile_cols]))
    weight = route_weight(parent_ids, block_maps, local)
    gathered[0], second_of_pair, weight = lax.optimization_barrier((gathered[0], second_of_pair, weight))
    second = rolled(jnp.stack([second, second_of_pair]), (h,))

    halves = []
    for f in range(local):
        partial = jnp.einsum("sk,mk->sm", gathered[f], masked[f], preferred_element_type=F32)
        halves.append(reduce_core(partial.astype(BF16).reshape(2, 2, slab, tile_rows), x, c))

    spread = ("h", "group") + ROW
    outgoing = jnp.stack([half.astype(BF16).reshape(2 * slab, tile_rows) for half in halves], axis=1)
    arrived = lax.all_to_all(outgoing, spread, split_axis=0, concat_axis=0, tiled=True)
    arrived = arrived[:slab].astype(F32) + arrived[slab:].astype(F32)
    arrived = arrived.astype(BF16).reshape(-1, tile_rows)
    extension = jnp.einsum("ij,jk->ik", weight, arrived, preferred_element_type=F32).astype(BF16)
    extension = extension.reshape(slab, local, tile_rows)
    extension = jnp.concatenate([extension, extension], axis=0)
    away = jnp.stack([pick(half, 1 - h).astype(BF16) for half in halves])
    away, extension = lax.optimization_barrier((away, extension))
    extension = lax.all_to_all(extension, spread, split_axis=0, concat_axis=0, tiled=True)
    received, extension = lax.optimization_barrier((shift(away, "h", 1), extension))
    combined = second.reshape(extension.shape).astype(F32) + extension.astype(F32)
    combined = combined.astype(BF16)

    nearer = ((x + ((c - x) & 1)) & 3) >> 1
    ordered = []
    for f in range(local):
        mine = combined[:, f, :].reshape(2, -1, own_rows, tile_rows)
        ordered.append(rolled(mine, (nearer, z)).reshape(2 * slab, tile_rows))
    everyone = lax.all_gather(jnp.stack(ordered), "c", axis=0)
    ordered = [rolled(everyone[:, f], (x & 1,)).reshape(4 * slab, tile_rows) for f in range(local)]

    def multiplied(f):
        product = jnp.einsum("sm,mk->sk", ordered[f], masked[f], preferred_element_type=F32)
        return product.astype(BF16)

    product_0 = multiplied(0)
    near_0 = first_step(first_pieces(product_0))
    product_1 = multiplied(1)
    pieces_1 = first_pieces(product_1)
    near_0, product_1, pieces_1 = lax.optimization_barrier((near_0, product_1, pieces_1))
    far_0 = second_step(product_0, near_0)
    near_1 = first_step(pieces_1)
    total_0 = last_step(product_0, near_0, far_0)
    far_1 = second_step(product_1, near_1)
    received, far_1 = lax.optimization_barrier((received, far_1))
    slabs = [pick(half, h) + received[f].astype(F32) for f, half in enumerate(halves)]
    sampled = jnp.stack([total.astype(BF16) for total in slabs], axis=1)
    total_1 = last_step(product_1, near_1, far_1)
    outs = [total_0.astype(BF16), total_1.astype(BF16)]
    return sampled, jnp.stack(outs, axis=1)


def solution(mesh):
    torus = Mesh(mesh.devices.reshape(mesh.shape["group"], 4, 4, 2, 2), DEVICES)
    in_specs = (P("group", ROW, COL), P(ROW, "group", COL), P(COL, "group", ROW), P(), P(), P())
    out_specs = (P(COL, "group", ROW), P(ROW, "group", COL))
    return jax.shard_map(
        shards, mesh=torus, in_specs=in_specs, out_specs=out_specs, check_vma=False
    )
```

```python
import jax
import jax.numpy as jnp
from jax import lax
from jax.experimental import pallas as pl
from jax.experimental.pallas import tpu as pltpu
from jax.sharding import Mesh
from jax.sharding import PartitionSpec as P

DEVICES = ("group", "x", "z", "h", "c")
ROW = ("x", "z")
COL = ("h", "c")
F32 = jnp.float32
BF16 = jnp.bfloat16


def shift(value, axis, by):
    n = lax.axis_size(axis)
    return lax.ppermute(value, axis, [(i, (i + by) % n) for i in range(n)])


def pick(value, index):
    return lax.dynamic_index_in_dim(value, index, 0, keepdims=False)


def rolled(value, starts):
    sizes = value.shape
    for axis in range(len(starts)):
        value = jnp.concatenate([value, value], axis=axis)
    starts = tuple(starts) + (0,) * (len(sizes) - len(starts))
    return lax.dynamic_slice(value, starts, sizes)


def gather_rows(columns):
    left = shift(columns, "x", 1)
    right = shift(columns, "x", -1)
    over = (shift(left[0], "x", 1), shift(right[1], "x", -1))
    return [jnp.concatenate([columns[f], over[f], left[f], right[f]], axis=0) for f in range(2)]


def mask_kernel(sizes_ref, origin_ref, fronts_ref, out_ref):
    tile = fronts_ref[...]
    size = sizes_ref[pl.program_id(0)]
    rows = origin_ref[0] + pl.program_id(1) * tile.shape[1] + lax.broadcasted_iota(jnp.int32, tile.shape, 1)
    cols = origin_ref[1] + lax.broadcasted_iota(jnp.int32, tile.shape, 2)
    out_ref[...] = jnp.where(jnp.maximum(rows, cols) < size, tile, jnp.zeros((), tile.dtype))


def masked_fronts(fronts, sizes, origin):
    local, rows, cols = fronts.shape
    step = 64
    spec = pl.BlockSpec((1, step, cols), lambda f, i: (f, i, 0))
    scalars = pl.BlockSpec(memory_space=pltpu.SMEM)
    return pl.pallas_call(
        mask_kernel,
        grid=(local, rows // step),
        in_specs=[scalars, scalars, spec],
        out_specs=spec,
        out_shape=jax.ShapeDtypeStruct(fronts.shape, fronts.dtype),
        compiler_params=pltpu.CompilerParams(vmem_limit_bytes=4 << 20),
    )(sizes, origin, fronts)


def reduce_core(partial, x, c):
    odd = (x - c) & 1
    received = shift(pick(partial, 1 - odd), "c", 1)
    total = pick(partial, odd).astype(F32) + received.astype(F32)
    return rolled(total, (((x - odd) & 3) >> 1,))


def first_pieces(product):
    block = product.shape[0] // 4
    half = block // 2
    to_right = product[block + half : 2 * block + half]
    to_left = jnp.concatenate([product[block : block + half], product[3 * block + half :]], axis=0)
    return to_right, to_left


def first_step(pieces):
    to_right, to_left = pieces
    return lax.optimization_barrier((shift(to_right, "x", 1), shift(to_left, "x", -1)))


def second_step(product, near):
    block = product.shape[0] // 4
    half = block // 2
    from_left, from_right = near
    over_right = product[2 * block + half : 3 * block].astype(F32) + from_left[:half].astype(F32)
    over_left = product[3 * block : 3 * block + half].astype(F32) + from_right[:half].astype(F32)
    over_right = shift(over_right.astype(BF16), "x", 1)
    over_left = shift(over_left.astype(BF16), "x", -1)
    return lax.optimization_barrier((over_right, over_left))


def last_step(product, near, far):
    block = product.shape[0] // 4
    half = block // 2
    rows = block // 4
    (from_left, from_right), (over_right, over_left) = near, far
    top = product[:half].astype(F32) + from_left[half:].astype(F32) + over_left.astype(F32)
    low = product[half:block].astype(F32) + from_right[half:].astype(F32) + over_right.astype(F32)
    own = jnp.concatenate([top, low], axis=0)
    total = own[:rows]
    for k in (1, 2, 3):
        piece = own[k * rows : (k + 1) * rows].astype(BF16)
        total = total + shift(piece, "z", k).astype(F32)
    return total


def route_weight(parent_ids, block_maps, local):
    count, blocks = block_maps.shape
    order = (count // local, local, blocks)
    parent = jnp.broadcast_to(parent_ids[:, None], block_maps.shape).reshape(order)
    parent = parent.transpose(0, 2, 1).reshape(1, -1)
    block = block_maps.reshape(order).transpose(0, 2, 1).reshape(1, -1)
    index = lax.broadcasted_iota(jnp.int32, (count * blocks, 1), 0)
    to_parent = index // (blocks * local) * local + index % local
    to_block = index // local % blocks
    return ((parent == to_parent) & (block == to_block)).astype(BF16)


def shards(fronts, samples, second_samples, front_sizes, parent_ids, block_maps):
    local, tile_rows, tile_cols = fronts.shape
    own_rows = samples.shape[0]
    slab = second_samples.shape[0]
    group, x, z, h, c = (lax.axis_index(axis) for axis in DEVICES)
    row = lax.axis_index(ROW)
    col = lax.axis_index(COL)

    mine = jnp.stack([samples[:, f, :] for f in range(local)])
    columns = lax.all_gather(mine, "z", axis=1, tiled=True)
    gathered = gather_rows(columns)
    sizes = lax.dynamic_slice_in_dim(front_sizes, group * local, local, 0)
    second, sizes, columns = lax.optimization_barrier((second_samples, sizes, columns))
    second_of_pair = shift(second, "h", 1)
    masked = masked_fronts(fronts, sizes, jnp.stack([row * tile_rows, col * tile_cols]))
    weight = route_weight(parent_ids, block_maps, local)
    gathered[0], second_of_pair, weight = lax.optimization_barrier((gathered[0], second_of_pair, weight))
    second = rolled(jnp.stack([second, second_of_pair]), (h,))

    halves = []
    for f in range(local):
        partial = jnp.einsum("sk,mk->sm", gathered[f], masked[f], preferred_element_type=F32)
        halves.append(reduce_core(partial.astype(BF16).reshape(2, 2, slab, tile_rows), x, c))

    spread = ("h", "group") + ROW
    outgoing = jnp.stack([half.astype(BF16).reshape(2 * slab, tile_rows) for half in halves], axis=1)
    arrived = lax.all_to_all(outgoing, spread, split_axis=0, concat_axis=0, tiled=True)
    arrived = arrived[:slab].astype(F32) + arrived[slab:].astype(F32)
    arrived = arrived.astype(BF16).reshape(-1, tile_rows)
    extension = jnp.einsum("ij,jk->ik", weight, arrived, preferred_element_type=F32).astype(BF16)
    extension = extension.reshape(slab, local, tile_rows)
    extension = jnp.concatenate([extension, extension], axis=0)
    extension = lax.all_to_all(extension, spread, split_axis=0, concat_axis=0, tiled=True)
    combined = second.reshape(extension.shape).astype(F32) + extension.astype(F32)
    combined = combined.astype(BF16)

    nearer = ((x + ((c - x) & 1)) & 3) >> 1
    ordered = []
    for f in range(local):
        mine = combined[:, f, :].reshape(2, -1, own_rows, tile_rows)
        ordered.append(rolled(mine, (nearer, z)).reshape(2 * slab, tile_rows))
    everyone = lax.all_gather(jnp.stack(ordered), "c", axis=0)
    ordered = [rolled(everyone[:, f], (x & 1,)).reshape(4 * slab, tile_rows) for f in range(local)]

    def multiplied(f):
        product = jnp.einsum("sm,mk->sk", ordered[f], masked[f], preferred_element_type=F32)
        return product.astype(BF16)

    product_0 = multiplied(0)
    product_0, *halves = lax.optimization_barrier((product_0, *halves))
    near_0 = first_step(first_pieces(product_0))
    product_1 = multiplied(1)
    pieces_1 = first_pieces(product_1)
    away = jnp.stack([pick(half, 1 - h).astype(BF16) for half in halves])
    away, pieces_1 = lax.optimization_barrier((away, pieces_1))
    received = shift(away, "h", 1)
    near_0, product_1, pieces_1, received = lax.optimization_barrier((near_0, product_1, pieces_1, received))
    far_0 = second_step(product_0, near_0)
    near_1 = first_step(pieces_1)
    total_0 = last_step(product_0, near_0, far_0)
    far_1 = second_step(product_1, near_1)
    received, far_1 = lax.optimization_barrier((received, far_1))
    slabs = [pick(half, h) + received[f].astype(F32) for f, half in enumerate(halves)]
    sampled = jnp.stack([total.astype(BF16) for total in slabs], axis=1)
    total_1 = last_step(product_1, near_1, far_1)
    outs = [total_0.astype(BF16), total_1.astype(BF16)]
    return sampled, jnp.stack(outs, axis=1)


def solution(mesh):
    torus = Mesh(mesh.devices.reshape(mesh.shape["group"], 4, 4, 2, 2), DEVICES)
    in_specs = (P("group", ROW, COL), P(ROW, "group", COL), P(COL, "group", ROW), P(), P(), P())
    out_specs = (P(COL, "group", ROW), P(ROW, "group", COL))
    return jax.shard_map(
        shards, mesh=torus, in_specs=in_specs, out_specs=out_specs, check_vma=False
    )
```

```python
import jax
import jax.numpy as jnp
from jax import lax
from jax.experimental import pallas as pl
from jax.experimental.pallas import tpu as pltpu
from jax.sharding import Mesh
from jax.sharding import PartitionSpec as P

DEVICES = ("group", "x", "z", "h", "c")
ROW = ("x", "z")
COL = ("h", "c")
F32 = jnp.float32
BF16 = jnp.bfloat16


def shift(value, axis, by):
    n = lax.axis_size(axis)
    return lax.ppermute(value, axis, [(i, (i + by) % n) for i in range(n)])


def pick(value, index):
    return lax.dynamic_index_in_dim(value, index, 0, keepdims=False)


def rolled(value, starts):
    sizes = value.shape
    for axis in range(len(starts)):
        value = jnp.concatenate([value, value], axis=axis)
    starts = tuple(starts) + (0,) * (len(sizes) - len(starts))
    return lax.dynamic_slice(value, starts, sizes)


def gather_rows(columns):
    left = shift(columns, "x", 1)
    right = shift(columns, "x", -1)
    over = (shift(left[0], "x", 1), shift(right[1], "x", -1))
    return [jnp.concatenate([columns[f], over[f], left[f], right[f]], axis=0) for f in range(2)]


def mask_kernel(sizes_ref, origin_ref, fronts_ref, out_ref):
    tile = fronts_ref[...]
    size = sizes_ref[pl.program_id(0)]
    rows = origin_ref[0] + pl.program_id(1) * tile.shape[1] + lax.broadcasted_iota(jnp.int32, tile.shape, 1)
    cols = origin_ref[1] + lax.broadcasted_iota(jnp.int32, tile.shape, 2)
    out_ref[...] = jnp.where(jnp.maximum(rows, cols) < size, tile, jnp.zeros((), tile.dtype))


def masked_fronts(fronts, sizes, origin):
    local, rows, cols = fronts.shape
    step = 64
    spec = pl.BlockSpec((1, step, cols), lambda f, i: (f, i, 0))
    scalars = pl.BlockSpec(memory_space=pltpu.SMEM)
    return pl.pallas_call(
        mask_kernel,
        grid=(local, rows // step),
        in_specs=[scalars, scalars, spec],
        out_specs=spec,
        out_shape=jax.ShapeDtypeStruct(fronts.shape, fronts.dtype),
        compiler_params=pltpu.CompilerParams(vmem_limit_bytes=4 << 20),
    )(sizes, origin, fronts)


def reduce_core(partial, x, c):
    odd = (x - c) & 1
    received = shift(pick(partial, 1 - odd), "c", 1)
    total = pick(partial, odd).astype(F32) + received.astype(F32)
    return rolled(total, (((x - odd) & 3) >> 1,))


def first_pieces(product):
    block = product.shape[0] // 4
    half = block // 2
    to_right = product[block + half : 2 * block + half]
    to_left = jnp.concatenate([product[block : block + half], product[3 * block + half :]], axis=0)
    return to_right, to_left


def first_step(pieces):
    to_right, to_left = pieces
    return lax.optimization_barrier((shift(to_right, "x", 1), shift(to_left, "x", -1)))


def second_pieces(product, near):
    block = product.shape[0] // 4
    half = block // 2
    from_left, from_right = near
    over_right = product[2 * block + half : 3 * block].astype(F32) + from_left[:half].astype(F32)
    over_left = product[3 * block : 3 * block + half].astype(F32) + from_right[:half].astype(F32)
    return over_right.astype(BF16), over_left.astype(BF16)


def second_step(pieces):
    over_right, over_left = pieces
    return lax.optimization_barrier((shift(over_right, "x", 1), shift(over_left, "x", -1)))


def last_step(product, near, far):
    block = product.shape[0] // 4
    half = block // 2
    rows = block // 4
    (from_left, from_right), (over_right, over_left) = near, far
    top = product[:half].astype(F32) + from_left[half:].astype(F32) + over_left.astype(F32)
    low = product[half:block].astype(F32) + from_right[half:].astype(F32) + over_right.astype(F32)
    own = jnp.concatenate([top, low], axis=0)
    total = own[:rows]
    for k in (1, 2, 3):
        piece = own[k * rows : (k + 1) * rows].astype(BF16)
        total = total + shift(piece, "z", k).astype(F32)
    return total


def route_weight(parent_ids, block_maps, local):
    count, blocks = block_maps.shape
    order = (count // local, local, blocks)
    parent = jnp.broadcast_to(parent_ids[:, None], block_maps.shape).reshape(order)
    parent = parent.transpose(0, 2, 1).reshape(1, -1)
    block = block_maps.reshape(order).transpose(0, 2, 1).reshape(1, -1)
    index = lax.broadcasted_iota(jnp.int32, (count * blocks, 1), 0)
    to_parent = index // (blocks * local) * local + index % local
    to_block = index // local % blocks
    return ((parent == to_parent) & (block == to_block)).astype(BF16)


def shards(fronts, samples, second_samples, front_sizes, parent_ids, block_maps):
    local, tile_rows, tile_cols = fronts.shape
    own_rows = samples.shape[0]
    slab = second_samples.shape[0]
    group, x, z, h, c = (lax.axis_index(axis) for axis in DEVICES)
    row = lax.axis_index(ROW)
    col = lax.axis_index(COL)

    mine = jnp.stack([samples[:, f, :] for f in range(local)])
    columns = lax.all_gather(mine, "z", axis=1, tiled=True)
    gathered = gather_rows(columns)
    sizes = lax.dynamic_slice_in_dim(front_sizes, group * local, local, 0)
    second, sizes, columns = lax.optimization_barrier((second_samples, sizes, columns))
    second_of_pair = shift(second, "h", 1)
    masked = masked_fronts(fronts, sizes, jnp.stack([row * tile_rows, col * tile_cols]))
    weight = route_weight(parent_ids, block_maps, local)
    gathered[0], second_of_pair, weight = lax.optimization_barrier((gathered[0], second_of_pair, weight))
    second = rolled(jnp.stack([second, second_of_pair]), (h,))

    halves = []
    for f in range(local):
        partial = jnp.einsum("sk,mk->sm", gathered[f], masked[f], preferred_element_type=F32)
        halves.append(reduce_core(partial.astype(BF16).reshape(2, 2, slab, tile_rows), x, c))

    away = jnp.stack([pick(half, 1 - h).astype(BF16) for half in halves])
    received = shift(away, "h", 1)
    slabs = [pick(half, h) + received[f].astype(F32) for f, half in enumerate(halves)]
    sampled = jnp.stack([total.astype(BF16) for total in slabs], axis=1)
    spread = ("group",) + ROW
    arrived = lax.all_to_all(sampled, spread, split_axis=0, concat_axis=0, tiled=True)
    arrived = arrived.reshape(-1, tile_rows)
    extension = jnp.einsum("ij,jk->ik", weight, arrived, preferred_element_type=F32).astype(BF16)
    extension = extension.reshape(slab, local, tile_rows)
    extension = jnp.concatenate([extension, extension], axis=0)
    extension = lax.all_to_all(extension, ("h",) + spread, split_axis=0, concat_axis=0, tiled=True)
    combined = second.reshape(extension.shape).astype(F32) + extension.astype(F32)
    combined = combined.astype(BF16)

    nearer = ((x + ((c - x) & 1)) & 3) >> 1
    ordered = []
    for f in range(local):
        mine = combined[:, f, :].reshape(2, -1, own_rows, tile_rows)
        ordered.append(rolled(mine, (nearer, z)).reshape(2 * slab, tile_rows))
    everyone = lax.all_gather(jnp.stack(ordered), "c", axis=0)
    ordered = [rolled(everyone[:, f], (x & 1,)).reshape(4 * slab, tile_rows) for f in range(local)]

    def multiplied(f):
        product = jnp.einsum("sm,mk->sk", ordered[f], masked[f], preferred_element_type=F32)
        return product.astype(BF16)

    product_0 = multiplied(0)
    near_0 = first_step(first_pieces(product_0))
    product_1 = multiplied(1)
    pieces_1 = first_pieces(product_1)
    near_0, product_1, pieces_1 = lax.optimization_barrier((near_0, product_1, pieces_1))
    far_0 = second_step(second_pieces(product_0, near_0))
    near_1 = first_step(pieces_1)
    total_0 = last_step(product_0, near_0, far_0)
    far_1 = second_step(second_pieces(product_1, near_1))
    total_1 = last_step(product_1, near_1, far_1)
    outs = [total_0.astype(BF16), total_1.astype(BF16)]
    return sampled, jnp.stack(outs, axis=1)


def solution(mesh):
    torus = Mesh(mesh.devices.reshape(mesh.shape["group"], 4, 4, 2, 2), DEVICES)
    in_specs = (P("group", ROW, COL), P(ROW, "group", COL), P(COL, "group", ROW), P(), P(), P())
    out_specs = (P(COL, "group", ROW), P(ROW, "group", COL))
    return jax.shard_map(
        shards, mesh=torus, in_specs=in_specs, out_specs=out_specs, check_vma=False
    )
```

```python
import jax
import jax.numpy as jnp
from jax import lax
from jax.experimental import pallas as pl
from jax.experimental.pallas import tpu as pltpu
from jax.sharding import Mesh
from jax.sharding import PartitionSpec as P

DEVICES = ("group", "x", "z", "h", "c")
ROW = ("x", "z")
COL = ("h", "c")
F32 = jnp.float32
BF16 = jnp.bfloat16


def shift(value, axis, by):
    n = lax.axis_size(axis)
    return lax.ppermute(value, axis, [(i, (i + by) % n) for i in range(n)])


def pick(value, index):
    return lax.dynamic_index_in_dim(value, index, 0, keepdims=False)


def rolled(value, starts):
    sizes = value.shape
    for axis in range(len(starts)):
        value = jnp.concatenate([value, value], axis=axis)
    starts = tuple(starts) + (0,) * (len(sizes) - len(starts))
    return lax.dynamic_slice(value, starts, sizes)


def gather_rows(columns):
    left = shift(columns, "x", 1)
    right = shift(columns, "x", -1)
    return left, right, (shift(left[0], "x", 1), shift(right[1], "x", -1))


def tile_of(cols):
    return min(cols, 512)


def sample_kernel(size_ref, place_ref, mine_ref, over_ref, left_ref, right_ref, front_ref, kept_ref, away_ref, total_ref):
    step = pl.program_id(0)
    rows = jnp.concatenate([mine_ref[0], over_ref[...], left_ref[0], right_ref[0]], axis=0)
    col = place_ref[1] + step * rows.shape[1] + lax.broadcasted_iota(jnp.int32, rows.shape, 1)
    rows = jnp.where(col < size_ref[0], rows, jnp.zeros((), BF16))
    part = lax.dot_general(rows, front_ref[0], (((1,), (1,)), ((), ())), preferred_element_type=F32)
    part = part.reshape(total_ref.shape)

    @pl.when(step == 0)
    def _():
        total_ref[...] = part

    @pl.when(step > 0)
    def _():
        total_ref[...] += part

    @pl.when(step == pl.num_programs(0) - 1)
    def _():
        row = place_ref[0] + lax.broadcasted_iota(jnp.int32, kept_ref.shape, 1)
        keep = row < size_ref[0]
        odd = place_ref[2]
        kept_ref[...] = jnp.where(keep, total_ref[odd], 0.0)
        away_ref[...] = jnp.where(keep, total_ref[1 - odd], 0.0).astype(BF16)


def sample_product(f, size, place, columns, over, left, right, fronts):
    _, rows, cols = fronts.shape
    count = columns.shape[1]
    tile = tile_of(cols)
    scalars = pl.BlockSpec(memory_space=pltpu.SMEM)
    of_front = pl.BlockSpec((1, count, tile), lambda j: (f, 0, j))
    half = pl.BlockSpec((2 * count, rows), lambda j: (0, 0))
    return pl.pallas_call(
        sample_kernel,
        grid=(cols // tile,),
        in_specs=[
            scalars,
            scalars,
            of_front,
            pl.BlockSpec((count, tile), lambda j: (0, j)),
            of_front,
            of_front,
            pl.BlockSpec((1, rows, tile), lambda j: (f, 0, j)),
        ],
        out_specs=[half, half],
        out_shape=[
            jax.ShapeDtypeStruct((2 * count, rows), F32),
            jax.ShapeDtypeStruct((2 * count, rows), BF16),
        ],
        scratch_shapes=[pltpu.VMEM((2, 2 * count, rows), F32)],
        compiler_params=pltpu.CompilerParams(vmem_limit_bytes=16 << 20),
    )(size, place, columns, over, left, right, pltpu.with_memory_space_constraint(fronts, pltpu.HBM))


def project_kernel(size_ref, place_ref, rows_ref, front_ref, right_ref, left_ref, rest_ref):
    first = place_ref[3]
    rows = jnp.concatenate([rows_ref[first, 0], rows_ref[1 - first, 0]], axis=0)
    product = jnp.dot(rows, front_ref[0], preferred_element_type=F32)
    col = place_ref[1] + pl.program_id(0) * product.shape[1] + lax.broadcasted_iota(jnp.int32, product.shape, 1)
    product = jnp.where(col < size_ref[0], product, 0.0).astype(BF16)
    half = right_ref.shape[0] // 2
    right_ref[...] = product[3 * half : 5 * half]
    left_ref[:half] = product[2 * half : 3 * half]
    left_ref[half:] = product[7 * half :]
    rest_ref[: 2 * half] = product[: 2 * half]
    rest_ref[2 * half :] = product[5 * half : 7 * half]


def project_product(f, size, place, everyone, fronts):
    _, rows, cols = fronts.shape
    count = everyone.shape[2]
    tile = tile_of(cols)
    scalars = pl.BlockSpec(memory_space=pltpu.SMEM)
    heights = (count // 2, count // 2, count)
    return pl.pallas_call(
        project_kernel,
        grid=(cols // tile,),
        in_specs=[
            scalars,
            scalars,
            pl.BlockSpec((2, 1, count, rows), lambda j: (0, f, 0, 0)),
            pl.BlockSpec((1, rows, tile), lambda j: (f, 0, j)),
        ],
        out_specs=[pl.BlockSpec((height, tile), lambda j: (0, j)) for height in heights],
        out_shape=[jax.ShapeDtypeStruct((height, cols), BF16) for height in heights],
        compiler_params=pltpu.CompilerParams(vmem_limit_bytes=16 << 20),
    )(size, place, everyone, pltpu.with_memory_space_constraint(fronts, pltpu.HBM))


def first_step(to_right, to_left):
    return lax.optimization_barrier((shift(to_right, "x", 1), shift(to_left, "x", -1)))


def second_pieces(rest, near):
    half = rest.shape[0] // 4
    from_left, from_right = near
    over_right = rest[2 * half : 3 * half].astype(F32) + from_left[:half].astype(F32)
    over_left = rest[3 * half :].astype(F32) + from_right[:half].astype(F32)
    return over_right.astype(BF16), over_left.astype(BF16)


def second_step(pieces):
    over_right, over_left = pieces
    return lax.optimization_barrier((shift(over_right, "x", 1), shift(over_left, "x", -1)))


def last_step(rest, near, far):
    half = rest.shape[0] // 4
    rows = half // 2
    (from_left, from_right), (over_right, over_left) = near, far
    top = rest[:half].astype(F32) + from_left[half:].astype(F32) + over_left.astype(F32)
    low = rest[half : 2 * half].astype(F32) + from_right[half:].astype(F32) + over_right.astype(F32)
    own = jnp.concatenate([top, low], axis=0)
    total = own[:rows]
    for k in (1, 2, 3):
        piece = own[k * rows : (k + 1) * rows].astype(BF16)
        total = total + shift(piece, "z", k).astype(F32)
    return total


def route_weight(parent_ids, block_maps, local):
    count, blocks = block_maps.shape
    order = (count // local, local, blocks)
    parent = jnp.broadcast_to(parent_ids[:, None], block_maps.shape).reshape(order)
    parent = parent.transpose(0, 2, 1).reshape(1, -1)
    block = block_maps.reshape(order).transpose(0, 2, 1).reshape(1, -1)
    index = lax.broadcasted_iota(jnp.int32, (count * blocks, 1), 0)
    to_parent = index // (blocks * local) * local + index % local
    to_block = index // local % blocks
    return ((parent == to_parent) & (block == to_block)).astype(BF16)


def shards(fronts, samples, second_samples, front_sizes, parent_ids, block_maps):
    local, tile_rows, tile_cols = fronts.shape
    own_rows = samples.shape[0]
    slab = second_samples.shape[0]
    group, x, z, h, c = (lax.axis_index(axis) for axis in DEVICES)
    row = lax.axis_index(ROW)
    col = lax.axis_index(COL)

    mine = jnp.stack([samples[:, f, :] for f in range(local)])
    columns = lax.all_gather(mine, "z", axis=1, tiled=True)
    left, right, over = gather_rows(columns)
    sizes = lax.dynamic_slice_in_dim(front_sizes, group * local, local, 0)
    second, _ = lax.optimization_barrier((second_samples, columns))
    second_of_pair = shift(second, "h", 1)
    odd = (x - c) & 1
    place = jnp.stack([row * tile_rows, col * tile_cols, odd, x & 1])
    weight = route_weight(parent_ids, block_maps, local)
    over_0, second_of_pair, weight = lax.optimization_barrier((over[0], second_of_pair, weight))
    over = (over_0, over[1])
    second = rolled(jnp.stack([second, second_of_pair]), (h,))

    halves = []
    for f in range(local):
        size = sizes[f : f + 1]
        kept, away = sample_product(f, size, place, columns, over[f], left, right, fronts)
        total = (kept + shift(away, "c", 1).astype(F32)).reshape(2, slab, tile_rows)
        halves.append(rolled(total, (((x - odd) & 3) >> 1,)))

    spread = ("h", "group") + ROW
    outgoing = jnp.stack([half.astype(BF16).reshape(2 * slab, tile_rows) for half in halves], axis=1)
    arrived = lax.all_to_all(outgoing, spread, split_axis=0, concat_axis=0, tiled=True)
    arrived = arrived[:slab].astype(F32) + arrived[slab:].astype(F32)
    arrived = arrived.astype(BF16).reshape(-1, tile_rows)
    extension = jnp.einsum("ij,jk->ik", weight, arrived, preferred_element_type=F32).astype(BF16)
    extension = extension.reshape(slab, local, tile_rows)
    extension = jnp.concatenate([extension, extension], axis=0)
    extension = lax.all_to_all(extension, spread, split_axis=0, concat_axis=0, tiled=True)
    combined = second.reshape(extension.shape).astype(F32) + extension.astype(F32)
    row_keep = row * tile_rows + lax.broadcasted_iota(jnp.int32, (local, tile_rows), 1) < sizes[:, None]
    combined = jnp.where(row_keep[None], combined, 0.0).astype(BF16)

    nearer = ((x + ((c - x) & 1)) & 3) >> 1
    ordered = []
    for f in range(local):
        mine = combined[:, f, :].reshape(2, -1, own_rows, tile_rows)
        ordered.append(rolled(mine, (nearer, z)).reshape(2 * slab, tile_rows))
    everyone = lax.all_gather(jnp.stack(ordered), "c", axis=0)
    right_0, left_0, rest_0 = project_product(0, sizes[:1], place, everyone, fronts)
    near_0 = first_step(right_0, left_0)
    everyone, right_0 = lax.optimization_barrier((everyone, right_0))
    right_1, left_1, rest_1 = project_product(1, sizes[1:], place, everyone, fronts)
    near_0, right_1, left_1 = lax.optimization_barrier((near_0, right_1, left_1))
    far_0 = second_step(second_pieces(rest_0, near_0))
    near_1 = first_step(right_1, left_1)
    away = jnp.stack([pick(half, 1 - h).astype(BF16) for half in halves])
    away, far_0 = lax.optimization_barrier((away, far_0))
    received = shift(away, "h", 1)
    total_0 = last_step(rest_0, near_0, far_0)
    far_1 = second_step(second_pieces(rest_1, near_1))
    received, far_1 = lax.optimization_barrier((received, far_1))
    slabs = [pick(half, h) + received[f].astype(F32) for f, half in enumerate(halves)]
    sampled = jnp.stack([total.astype(BF16) for total in slabs], axis=1)
    total_1 = last_step(rest_1, near_1, far_1)
    outs = [total_0.astype(BF16), total_1.astype(BF16)]
    return sampled, jnp.stack(outs, axis=1)


def solution(mesh):
    torus = Mesh(mesh.devices.reshape(mesh.shape["group"], 4, 4, 2, 2), DEVICES)
    in_specs = (P("group", ROW, COL), P(ROW, "group", COL), P(COL, "group", ROW), P(), P(), P())
    out_specs = (P(COL, "group", ROW), P(ROW, "group", COL))
    return jax.shard_map(
        shards, mesh=torus, in_specs=in_specs, out_specs=out_specs, check_vma=False
    )
```

```python
import jax
import jax.numpy as jnp
from jax import lax
from jax.experimental import pallas as pl
from jax.experimental.pallas import tpu as pltpu
from jax.sharding import Mesh
from jax.sharding import PartitionSpec as P

DEVICES = ("group", "x", "z", "h", "c")
ROW = ("x", "z")
COL = ("h", "c")
F32 = jnp.float32
BF16 = jnp.bfloat16


def shift(value, axis, by):
    n = lax.axis_size(axis)
    return lax.ppermute(value, axis, [(i, (i + by) % n) for i in range(n)])


def pick(value, index):
    return lax.dynamic_index_in_dim(value, index, 0, keepdims=False)


def rolled(value, starts):
    sizes = value.shape
    for axis in range(len(starts)):
        value = jnp.concatenate([value, value], axis=axis)
    starts = tuple(starts) + (0,) * (len(sizes) - len(starts))
    return lax.dynamic_slice(value, starts, sizes)


def gather_rows(columns):
    left = shift(columns, "x", 1)
    right = shift(columns, "x", -1)
    over = (shift(left[0], "x", 1), shift(right[1], "x", -1))
    return [jnp.concatenate([columns[f], over[f], left[f], right[f]], axis=0) for f in range(2)]


def mask_kernel(sizes_ref, origin_ref, fronts_ref, out_ref):
    tile = fronts_ref[...]
    size = sizes_ref[pl.program_id(0)]
    rows = origin_ref[0] + pl.program_id(1) * tile.shape[1] + lax.broadcasted_iota(jnp.int32, tile.shape, 1)
    cols = origin_ref[1] + lax.broadcasted_iota(jnp.int32, tile.shape, 2)
    out_ref[...] = jnp.where(jnp.maximum(rows, cols) < size, tile, jnp.zeros((), tile.dtype))


def masked_fronts(fronts, sizes, origin):
    local, rows, cols = fronts.shape
    step = 64
    spec = pl.BlockSpec((1, step, cols), lambda f, i: (f, i, 0))
    scalars = pl.BlockSpec(memory_space=pltpu.SMEM)
    return pl.pallas_call(
        mask_kernel,
        grid=(local, rows // step),
        in_specs=[scalars, scalars, spec],
        out_specs=spec,
        out_shape=jax.ShapeDtypeStruct(fronts.shape, fronts.dtype),
        compiler_params=pltpu.CompilerParams(vmem_limit_bytes=4 << 20),
    )(sizes, origin, fronts)


def reduce_core(partial, x, c):
    odd = (x - c) & 1
    received = shift(pick(partial, 1 - odd), "c", 1)
    total = pick(partial, odd).astype(F32) + received.astype(F32)
    return rolled(total, (((x - odd) & 3) >> 1,))


def first_pieces(product):
    block = product.shape[0] // 4
    half = block // 2
    to_right = product[block + half : 2 * block + half]
    to_left = jnp.concatenate([product[block : block + half], product[3 * block + half :]], axis=0)
    return to_right, to_left


def first_step(products):
    pieces = [first_pieces(product) for product in products]
    to_right = jnp.concatenate([piece[0] for piece in pieces], axis=0)
    to_left = jnp.concatenate([piece[1] for piece in pieces], axis=0)
    return shift(to_right, "x", 1), shift(to_left, "x", -1)


def second_pieces(product, near):
    block = product.shape[0] // 4
    half = block // 2
    from_left, from_right = near
    over_right = product[2 * block + half : 3 * block].astype(F32) + from_left[:half].astype(F32)
    over_left = product[3 * block : 3 * block + half].astype(F32) + from_right[:half].astype(F32)
    return over_right.astype(BF16), over_left.astype(BF16)


def second_step(pieces):
    over_right, over_left = pieces
    return lax.optimization_barrier((shift(over_right, "x", 1), shift(over_left, "x", -1)))


def own_rows_of(product, near, far):
    block = product.shape[0] // 4
    half = block // 2
    (from_left, from_right), (over_right, over_left) = near, far
    top = product[:half].astype(F32) + from_left[half:].astype(F32) + over_left.astype(F32)
    low = product[half:block].astype(F32) + from_right[half:].astype(F32) + over_right.astype(F32)
    own = jnp.concatenate([top, low], axis=0).reshape(4, -1, product.shape[1])
    return own[0], [own[k].astype(BF16) for k in (1, 2, 3)]


def last_step(own, pieces):
    for k, piece in enumerate(pieces):
        own = own + shift(piece, "z", k + 1).astype(F32)
    return own


def route_weight(parent_ids, block_maps, local):
    count, blocks = block_maps.shape
    order = (count // local, local, blocks)
    parent = jnp.broadcast_to(parent_ids[:, None], block_maps.shape).reshape(order)
    parent = parent.transpose(0, 2, 1).reshape(1, -1)
    block = block_maps.reshape(order).transpose(0, 2, 1).reshape(1, -1)
    index = lax.broadcasted_iota(jnp.int32, (count * blocks, 1), 0)
    to_parent = index // (blocks * local) * local + index % local
    to_block = index // local % blocks
    return ((parent == to_parent) & (block == to_block)).astype(BF16)


def shards(fronts, samples, second_samples, front_sizes, parent_ids, block_maps):
    local, tile_rows, tile_cols = fronts.shape
    own_rows = samples.shape[0]
    slab = second_samples.shape[0]
    group, x, z, h, c = (lax.axis_index(axis) for axis in DEVICES)
    row = lax.axis_index(ROW)
    col = lax.axis_index(COL)

    mine = jnp.stack([samples[:, f, :] for f in range(local)])
    columns = lax.all_gather(mine, "z", axis=1, tiled=True)
    gathered = gather_rows(columns)
    sizes = lax.dynamic_slice_in_dim(front_sizes, group * local, local, 0)
    second, sizes, columns = lax.optimization_barrier((second_samples, sizes, columns))
    second_of_pair = shift(second, "h", 1)
    masked = masked_fronts(fronts, sizes, jnp.stack([row * tile_rows, col * tile_cols]))
    weight = route_weight(parent_ids, block_maps, local)
    first = jnp.broadcast_to(h == 0, (1, tile_rows))
    gathered[0], second_of_pair, weight, first = lax.optimization_barrier(
        (gathered[0], second_of_pair, weight, first)
    )
    second = rolled(jnp.stack([second, second_of_pair]), (h,))

    halves = []
    for f in range(local):
        partial = jnp.einsum("sk,mk->sm", gathered[f], masked[f], preferred_element_type=F32)
        halves.append(reduce_core(partial.astype(BF16).reshape(2, 2, slab, tile_rows), x, c))

    spread = ("h", "group") + ROW
    outgoing = jnp.stack([half.astype(BF16).reshape(2 * slab, tile_rows) for half in halves], axis=1)
    arrived = lax.all_to_all(outgoing, spread, split_axis=0, concat_axis=0, tiled=True)
    arrived = arrived[:slab].astype(F32) + arrived[slab:].astype(F32)
    arrived = arrived.astype(BF16).reshape(-1, tile_rows)
    extension = jnp.einsum("ij,jk->ik", weight, arrived, preferred_element_type=F32).astype(BF16)
    extension = extension.reshape(slab, local, tile_rows)
    extension = jnp.concatenate([extension, extension], axis=0)
    extension = lax.all_to_all(extension, spread, split_axis=0, concat_axis=0, tiled=True)
    combined = second.reshape(extension.shape).astype(F32) + extension.astype(F32)
    combined = combined.astype(BF16)

    nearer = ((x + ((c - x) & 1)) & 3) >> 1
    ordered = []
    for f in range(local):
        mine = combined[:, f, :].reshape(2, -1, own_rows, tile_rows)
        ordered.append(rolled(mine, (nearer, z)).reshape(2 * slab, tile_rows))
    everyone = lax.all_gather(jnp.stack(ordered), "c", axis=0)
    ordered = [rolled(everyone[:, f], (x & 1,)).reshape(4 * slab, tile_rows) for f in range(local)]

    def multiplied(f):
        product = jnp.einsum("sm,mk->sk", ordered[f], masked[f], preferred_element_type=F32)
        return product.astype(BF16)

    products = [multiplied(f) for f in range(local)]
    products[0], *halves = lax.optimization_barrier((products[0], *halves))
    from_left, from_right = first_step(products)
    away = jnp.stack([jnp.where(first, half[1], half[0]).astype(BF16) for half in halves])
    away, _ = lax.optimization_barrier((away, products[1]))
    received = shift(away, "h", 1)
    from_left, from_right, received = lax.optimization_barrier((from_left, from_right, received))
    near = [(from_left[f * slab : (f + 1) * slab], from_right[f * slab : (f + 1) * slab]) for f in range(local)]
    far_0 = second_step(second_pieces(products[0], near[0]))
    passed_1 = second_pieces(products[1], near[1])
    far_1 = second_step(passed_1)
    far_0, _ = lax.optimization_barrier((far_0, passed_1))
    own_0, pieces_0 = own_rows_of(products[0], near[0], far_0)
    far_1, _ = lax.optimization_barrier((far_1, pieces_0))
    own_1, pieces_1 = own_rows_of(products[1], near[1], far_1)
    total_0 = last_step(own_0, pieces_0)
    received, _ = lax.optimization_barrier((received, pieces_1))
    slabs = [jnp.where(first, half[0], half[1]) + received[f].astype(F32) for f, half in enumerate(halves)]
    sampled = jnp.stack([total.astype(BF16) for total in slabs], axis=1)
    total_1 = last_step(own_1, pieces_1)
    outs = [total_0.astype(BF16), total_1.astype(BF16)]
    return sampled, jnp.stack(outs, axis=1)


def solution(mesh):
    torus = Mesh(mesh.devices.reshape(mesh.shape["group"], 4, 4, 2, 2), DEVICES)
    in_specs = (P("group", ROW, COL), P(ROW, "group", COL), P(COL, "group", ROW), P(), P(), P())
    out_specs = (P(COL, "group", ROW), P(ROW, "group", COL))
    return jax.shard_map(
        shards, mesh=torus, in_specs=in_specs, out_specs=out_specs, check_vma=False
    )
```

```python
import jax
import jax.numpy as jnp
from jax import lax
from jax.experimental import pallas as pl
from jax.experimental.pallas import tpu as pltpu
from jax.sharding import Mesh
from jax.sharding import PartitionSpec as P

DEVICES = ("group", "x", "z", "h", "c")
ROW = ("x", "z")
COL = ("h", "c")
F32 = jnp.float32
BF16 = jnp.bfloat16


def shift(value, axis, by):
    n = lax.axis_size(axis)
    return lax.ppermute(value, axis, [(i, (i + by) % n) for i in range(n)])


def pick(value, index):
    return lax.dynamic_index_in_dim(value, index, 0, keepdims=False)


def rolled(value, starts):
    sizes = value.shape
    for axis in range(len(starts)):
        value = jnp.concatenate([value, value], axis=axis)
    starts = tuple(starts) + (0,) * (len(sizes) - len(starts))
    return lax.dynamic_slice(value, starts, sizes)


def gather_rows(columns):
    left = shift(columns, "x", 1)
    right = shift(columns, "x", -1)
    over = (shift(left[0], "x", 1), shift(right[1], "x", -1))
    return [jnp.concatenate([columns[f], over[f], left[f], right[f]], axis=0) for f in range(2)]


def mask_kernel(sizes_ref, origin_ref, fronts_ref, out_ref):
    tile = fronts_ref[...]
    size = sizes_ref[pl.program_id(0)]
    rows = origin_ref[0] + pl.program_id(1) * tile.shape[1] + lax.broadcasted_iota(jnp.int32, tile.shape, 1)
    cols = origin_ref[1] + lax.broadcasted_iota(jnp.int32, tile.shape, 2)
    out_ref[...] = jnp.where(jnp.maximum(rows, cols) < size, tile, jnp.zeros((), tile.dtype))


def masked_fronts(fronts, sizes, origin):
    local, rows, cols = fronts.shape
    step = 64
    spec = pl.BlockSpec((1, step, cols), lambda f, i: (f, i, 0))
    scalars = pl.BlockSpec(memory_space=pltpu.SMEM)
    return pl.pallas_call(
        mask_kernel,
        grid=(local, rows // step),
        in_specs=[scalars, scalars, spec],
        out_specs=spec,
        out_shape=jax.ShapeDtypeStruct(fronts.shape, fronts.dtype),
        compiler_params=pltpu.CompilerParams(vmem_limit_bytes=4 << 20),
    )(sizes, origin, fronts)


def reduce_core(partial, x, c):
    odd = (x - c) & 1
    received = shift(pick(partial, 1 - odd), "c", 1)
    total = pick(partial, odd).astype(F32) + received.astype(F32)
    return rolled(total, (((x - odd) & 3) >> 1,))


def first_pieces(product):
    block = product.shape[0] // 4
    half = block // 2
    to_right = product[block + half : 2 * block + half]
    to_left = jnp.concatenate([product[block : block + half], product[3 * block + half :]], axis=0)
    return to_right, to_left


def first_step(pieces):
    to_right, to_left = pieces
    return lax.optimization_barrier((shift(to_right, "x", 1), shift(to_left, "x", -1)))


def second_pieces(product, near):
    block = product.shape[0] // 4
    half = block // 2
    from_left, from_right = near
    over_right = product[2 * block + half : 3 * block].astype(F32) + from_left[:half].astype(F32)
    over_left = product[3 * block : 3 * block + half].astype(F32) + from_right[:half].astype(F32)
    return over_right.astype(BF16), over_left.astype(BF16)


def second_step(pieces):
    over_right, over_left = pieces
    return lax.optimization_barrier((shift(over_right, "x", 1), shift(over_left, "x", -1)))


def last_step(product, near, far):
    block = product.shape[0] // 4
    half = block // 2
    rows = block // 4
    (from_left, from_right), (over_right, over_left) = near, far
    top = product[:half].astype(F32) + from_left[half:].astype(F32) + over_left.astype(F32)
    low = product[half:block].astype(F32) + from_right[half:].astype(F32) + over_right.astype(F32)
    own = jnp.concatenate([top, low], axis=0)
    total = own[:rows]
    for k in (1, 2, 3):
        piece = own[k * rows : (k + 1) * rows].astype(BF16)
        total = total + shift(piece, "z", k).astype(F32)
    return total


def route_weight(parent_ids, block_maps, local):
    count, blocks = block_maps.shape
    order = (count // local, local, blocks)
    parent = jnp.broadcast_to(parent_ids[:, None], block_maps.shape).reshape(order)
    parent = parent.transpose(0, 2, 1).reshape(1, -1)
    block = block_maps.reshape(order).transpose(0, 2, 1).reshape(1, -1)
    index = lax.broadcasted_iota(jnp.int32, (count * blocks, 1), 0)
    to_parent = index // (blocks * local) * local + index % local
    to_block = index // local % blocks
    return ((parent == to_parent) & (block == to_block)).astype(BF16)


def shards(fronts, samples, second_samples, front_sizes, parent_ids, block_maps):
    local, tile_rows, tile_cols = fronts.shape
    own_rows = samples.shape[0]
    slab = second_samples.shape[0]
    group, x, z, h, c = (lax.axis_index(axis) for axis in DEVICES)
    row = lax.axis_index(ROW)
    col = lax.axis_index(COL)

    mine = jnp.stack([samples[:, f, :] for f in range(local)])
    columns = lax.all_gather(mine, "z", axis=1, tiled=True)
    gathered = gather_rows(columns)
    sizes = lax.dynamic_slice_in_dim(front_sizes, group * local, local, 0)
    second, sizes, columns = lax.optimization_barrier((second_samples, sizes, columns))
    second_of_pair = shift(second, "h", 1)
    masked = masked_fronts(fronts, sizes, jnp.stack([row * tile_rows, col * tile_cols]))
    weight = route_weight(parent_ids, block_maps, local)
    first = jnp.broadcast_to(h == 0, (1, tile_rows))
    gathered[0], second_of_pair, weight, first = lax.optimization_barrier(
        (gathered[0], second_of_pair, weight, first)
    )
    second = rolled(jnp.stack([second, second_of_pair]), (h,))

    halves = []
    for f in range(local):
        partial = jnp.einsum("sk,mk->sm", gathered[f], masked[f], preferred_element_type=F32)
        halves.append(reduce_core(partial.astype(BF16).reshape(2, 2, slab, tile_rows), x, c))

    spread = ("h", "group") + ROW
    outgoing = jnp.stack([half.astype(BF16).reshape(2 * slab, tile_rows) for half in halves], axis=1)
    arrived = lax.all_to_all(outgoing, spread, split_axis=0, concat_axis=0, tiled=True)
    arrived = arrived[:slab].astype(F32) + arrived[slab:].astype(F32)
    arrived = arrived.astype(BF16).reshape(-1, tile_rows)
    extension = jnp.einsum("ij,jk->ik", weight, arrived, preferred_element_type=F32).astype(BF16)
    extension = extension.reshape(slab, local, tile_rows)
    extension = jnp.concatenate([extension, extension], axis=0)
    extension = lax.all_to_all(extension, spread, split_axis=0, concat_axis=0, tiled=True)
    combined = second.reshape(extension.shape).astype(F32) + extension.astype(F32)
    combined = combined.astype(BF16)

    nearer = ((x + ((c - x) & 1)) & 3) >> 1
    ordered = []
    for f in range(local):
        mine = combined[:, f, :].reshape(2, -1, own_rows, tile_rows)
        ordered.append(rolled(mine, (nearer, z)).reshape(2 * slab, tile_rows))
    everyone = lax.all_gather(jnp.stack(ordered), "c", axis=0)
    ordered = [rolled(everyone[:, f], (x & 1,)).reshape(4 * slab, tile_rows) for f in range(local)]

    def multiplied(f):
        product = jnp.einsum("sm,mk->sk", ordered[f], masked[f], preferred_element_type=F32)
        return product.astype(BF16)

    product_0 = multiplied(0)
    product_0, *halves = lax.optimization_barrier((product_0, *halves))
    pieces_0 = first_pieces(product_0)
    near_0 = first_step(pieces_0)
    ordered[1], _ = lax.optimization_barrier((ordered[1], pieces_0))
    product_1 = multiplied(1)
    pieces_1 = first_pieces(product_1)
    away = [jnp.where(first, half[1], half[0]).astype(BF16) for half in halves]
    away[0], _ = lax.optimization_barrier((away[0], pieces_0))
    received_0 = shift(away[0], "h", 1)
    near_0, product_1, pieces_1, received_0 = lax.optimization_barrier((near_0, product_1, pieces_1, received_0))
    far_0 = second_step(second_pieces(product_0, near_0))
    near_1 = first_step(pieces_1)
    total_0 = last_step(product_0, near_0, far_0)
    passed_1 = second_pieces(product_1, near_1)
    far_1 = second_step(passed_1)
    away[1], _ = lax.optimization_barrier((away[1], passed_1))
    received_1 = shift(away[1], "h", 1)
    received_1, far_1 = lax.optimization_barrier((received_1, far_1))
    slabs = [
        jnp.where(first, half[0], half[1]) + received.astype(F32)
        for half, received in zip(halves, (received_0, received_1))
    ]
    sampled = jnp.stack([total.astype(BF16) for total in slabs], axis=1)
    total_1 = last_step(product_1, near_1, far_1)
    outs = [total_0.astype(BF16), total_1.astype(BF16)]
    return sampled, jnp.stack(outs, axis=1)


def solution(mesh):
    torus = Mesh(mesh.devices.reshape(mesh.shape["group"], 4, 4, 2, 2), DEVICES)
    in_specs = (P("group", ROW, COL), P(ROW, "group", COL), P(COL, "group", ROW), P(), P(), P())
    out_specs = (P(COL, "group", ROW), P(ROW, "group", COL))
    return jax.shard_map(
        shards, mesh=torus, in_specs=in_specs, out_specs=out_specs, check_vma=False
    )
```

```python
import jax
import jax.numpy as jnp
from jax import lax
from jax.experimental import pallas as pl
from jax.experimental.pallas import tpu as pltpu
from jax.sharding import Mesh
from jax.sharding import PartitionSpec as P

DEVICES = ("group", "x", "z", "h", "c")
ROW = ("x", "z")
COL = ("h", "c")
F32 = jnp.float32
BF16 = jnp.bfloat16


def shift(value, axis, by):
    n = lax.axis_size(axis)
    return lax.ppermute(value, axis, [(i, (i + by) % n) for i in range(n)])


def pick(value, index):
    return lax.dynamic_index_in_dim(value, index, 0, keepdims=False)


def rolled(value, starts):
    sizes = value.shape
    for axis in range(len(starts)):
        value = jnp.concatenate([value, value], axis=axis)
    starts = tuple(starts) + (0,) * (len(sizes) - len(starts))
    return lax.dynamic_slice(value, starts, sizes)


def gather_rows(columns):
    left = shift(columns, "x", 1)
    right = shift(columns, "x", -1)
    over = (shift(left[0], "x", 1), shift(right[1], "x", -1))
    return [jnp.concatenate([columns[f], over[f], left[f], right[f]], axis=0) for f in range(2)]


def mask_kernel(sizes_ref, origin_ref, fronts_ref, out_ref):
    tile = fronts_ref[...]
    size = sizes_ref[pl.program_id(0)]
    rows = origin_ref[0] + pl.program_id(1) * tile.shape[1] + lax.broadcasted_iota(jnp.int32, tile.shape, 1)
    cols = origin_ref[1] + lax.broadcasted_iota(jnp.int32, tile.shape, 2)
    out_ref[...] = jnp.where(jnp.maximum(rows, cols) < size, tile, jnp.zeros((), tile.dtype))


def masked_fronts(fronts, sizes, origin):
    local, rows, cols = fronts.shape
    step = 64
    spec = pl.BlockSpec((1, step, cols), lambda f, i: (f, i, 0))
    scalars = pl.BlockSpec(memory_space=pltpu.SMEM)
    return pl.pallas_call(
        mask_kernel,
        grid=(local, rows // step),
        in_specs=[scalars, scalars, spec],
        out_specs=spec,
        out_shape=jax.ShapeDtypeStruct(fronts.shape, fronts.dtype),
        compiler_params=pltpu.CompilerParams(vmem_limit_bytes=4 << 20),
    )(sizes, origin, fronts)


def reduce_core(partial, x, c):
    odd = (x - c) & 1
    received = shift(pick(partial, 1 - odd), "c", 1)
    total = pick(partial, odd).astype(F32) + received.astype(F32)
    return rolled(total, (((x - odd) & 3) >> 1,))


def first_pieces(product):
    block = product.shape[0] // 4
    half = block // 2
    to_right = product[block + half : 2 * block + half]
    to_left = jnp.concatenate([product[block : block + half], product[3 * block + half :]], axis=0)
    return to_right, to_left


def first_step(pieces):
    to_right, to_left = pieces
    return lax.optimization_barrier((shift(to_right, "x", 1), shift(to_left, "x", -1)))


def second_pieces(product, near):
    block = product.shape[0] // 4
    half = block // 2
    from_left, from_right = near
    over_right = product[2 * block + half : 3 * block].astype(F32) + from_left[:half].astype(F32)
    over_left = product[3 * block : 3 * block + half].astype(F32) + from_right[:half].astype(F32)
    return over_right.astype(BF16), over_left.astype(BF16)


def second_step(pieces):
    over_right, over_left = pieces
    return lax.optimization_barrier((shift(over_right, "x", 1), shift(over_left, "x", -1)))


def last_step(product, near, far):
    block = product.shape[0] // 4
    half = block // 2
    rows = block // 4
    (from_left, from_right), (over_right, over_left) = near, far
    top = product[:half].astype(F32) + from_left[half:].astype(F32) + over_left.astype(F32)
    low = product[half:block].astype(F32) + from_right[half:].astype(F32) + over_right.astype(F32)
    own = jnp.concatenate([top, low], axis=0)
    total = own[:rows]
    for k in (1, 2, 3):
        piece = own[k * rows : (k + 1) * rows].astype(BF16)
        total = total + shift(piece, "z", k).astype(F32)
    return total


def route_weight(parent_ids, block_maps, local):
    count, blocks = block_maps.shape
    order = (count // local, local, blocks)
    parent = jnp.broadcast_to(parent_ids[:, None], block_maps.shape).reshape(order)
    parent = parent.transpose(0, 2, 1).reshape(1, -1)
    block = block_maps.reshape(order).transpose(0, 2, 1).reshape(1, -1)
    index = lax.broadcasted_iota(jnp.int32, (count * blocks, 1), 0)
    to_parent = index // (blocks * local) * local + index % local
    to_block = index // local % blocks
    return ((parent == to_parent) & (block == to_block)).astype(BF16)


def shards(fronts, samples, second_samples, front_sizes, parent_ids, block_maps):
    local, tile_rows, tile_cols = fronts.shape
    own_rows = samples.shape[0]
    slab = second_samples.shape[0]
    group, x, z, h, c = (lax.axis_index(axis) for axis in DEVICES)
    row = lax.axis_index(ROW)
    col = lax.axis_index(COL)

    mine = jnp.stack([samples[:, f, :] for f in range(local)])
    columns = lax.all_gather(mine, "z", axis=1, tiled=True)
    gathered = gather_rows(columns)
    sizes = lax.dynamic_slice_in_dim(front_sizes, group * local, local, 0)
    second, sizes, columns = lax.optimization_barrier((second_samples, sizes, columns))
    second_of_pair = shift(second, "h", 1)
    masked = masked_fronts(fronts, sizes, jnp.stack([row * tile_rows, col * tile_cols]))
    weight = route_weight(parent_ids, block_maps, local)
    first = jnp.broadcast_to(h == 0, (1, tile_rows))
    gathered[0], second_of_pair, weight, first = lax.optimization_barrier(
        (gathered[0], second_of_pair, weight, first)
    )
    second = rolled(jnp.stack([second, second_of_pair]), (h,))

    halves = []
    for f in range(local):
        partial = jnp.einsum("sk,mk->sm", gathered[f], masked[f], preferred_element_type=F32)
        halves.append(reduce_core(partial.astype(BF16).reshape(2, 2, slab, tile_rows), x, c))

    spread = ("h", "group") + ROW
    outgoing = jnp.stack([half.astype(BF16).reshape(2 * slab, tile_rows) for half in halves], axis=1)
    arrived = lax.all_to_all(outgoing, spread, split_axis=0, concat_axis=0, tiled=True)
    arrived = arrived[:slab].astype(F32) + arrived[slab:].astype(F32)
    arrived = arrived.astype(BF16).reshape(-1, tile_rows)
    extension = jnp.einsum("ij,jk->ik", weight, arrived, preferred_element_type=F32).astype(BF16)
    extension = extension.reshape(slab, local, tile_rows)
    extension = jnp.concatenate([extension, extension], axis=0)
    extension = lax.all_to_all(extension, spread, split_axis=0, concat_axis=0, tiled=True)
    combined = second.reshape(extension.shape).astype(F32) + extension.astype(F32)
    combined = combined.astype(BF16)

    nearer = ((x + ((c - x) & 1)) & 3) >> 1
    ordered = []
    for f in range(local):
        mine = combined[:, f, :].reshape(2, -1, own_rows, tile_rows)
        ordered.append(rolled(mine, (nearer, z)).reshape(2 * slab, tile_rows))
    everyone = lax.all_gather(jnp.stack(ordered), "c", axis=0)
    ordered = [rolled(everyone[:, f], (x & 1,)).reshape(4 * slab, tile_rows) for f in range(local)]

    def multiplied(f):
        product = jnp.einsum("sm,mk->sk", ordered[f], masked[f], preferred_element_type=F32)
        return product.astype(BF16)

    product_0 = multiplied(0)
    product_0, *halves = lax.optimization_barrier((product_0, *halves))
    pieces_0 = first_pieces(product_0)
    near_0 = first_step(pieces_0)
    ordered[1], _ = lax.optimization_barrier((ordered[1], pieces_0))
    product_1 = multiplied(1)
    pieces_1 = first_pieces(product_1)
    away = jnp.stack([jnp.where(first, half[1], half[0]).astype(BF16) for half in halves])
    away, _ = lax.optimization_barrier((away, pieces_0))
    received = shift(away, "h", 1)
    near_0, product_1, pieces_1, received = lax.optimization_barrier((near_0, product_1, pieces_1, received))
    far_0 = second_step(second_pieces(product_0, near_0))
    near_1 = first_step(pieces_1)
    total_0 = last_step(product_0, near_0, far_0)
    passed_1 = second_pieces(product_1, near_1)
    far_1 = second_step(passed_1)
    received, _ = lax.optimization_barrier((received, far_1))
    slabs = [jnp.where(first, half[0], half[1]) + received[f].astype(F32) for f, half in enumerate(halves)]
    sampled = jnp.stack([total.astype(BF16) for total in slabs], axis=1)
    total_1 = last_step(product_1, near_1, far_1)
    outs = [total_0.astype(BF16), total_1.astype(BF16)]
    return sampled, jnp.stack(outs, axis=1)


def solution(mesh):
    torus = Mesh(mesh.devices.reshape(mesh.shape["group"], 4, 4, 2, 2), DEVICES)
    in_specs = (P("group", ROW, COL), P(ROW, "group", COL), P(COL, "group", ROW), P(), P(), P())
    out_specs = (P(COL, "group", ROW), P(ROW, "group", COL))
    return jax.shard_map(
        shards, mesh=torus, in_specs=in_specs, out_specs=out_specs, check_vma=False
    )
```

```python
import jax
import jax.numpy as jnp
from jax import lax
from jax.experimental import pallas as pl
from jax.experimental.pallas import tpu as pltpu
from jax.sharding import Mesh
from jax.sharding import PartitionSpec as P

DEVICES = ("group", "x", "z", "h", "c")
ROW = ("x", "z")
COL = ("h", "c")
F32 = jnp.float32
BF16 = jnp.bfloat16


def shift(value, axis, by):
    n = lax.axis_size(axis)
    return lax.ppermute(value, axis, [(i, (i + by) % n) for i in range(n)])


def pick(value, index):
    return lax.dynamic_index_in_dim(value, index, 0, keepdims=False)


def rolled(value, starts):
    sizes = value.shape
    for axis in range(len(starts)):
        value = jnp.concatenate([value, value], axis=axis)
    starts = tuple(starts) + (0,) * (len(sizes) - len(starts))
    return lax.dynamic_slice(value, starts, sizes)


def gather_rows(columns):
    left = shift(columns, "x", 1)
    right = shift(columns, "x", -1)
    over = (shift(left[0], "x", 1), shift(right[1], "x", -1))
    return [jnp.concatenate([columns[f], over[f], left[f], right[f]], axis=0) for f in range(2)]


def mask_kernel(sizes_ref, origin_ref, fronts_ref, out_ref):
    tile = fronts_ref[...]
    size = sizes_ref[pl.program_id(0)]
    rows = origin_ref[0] + pl.program_id(1) * tile.shape[1] + lax.broadcasted_iota(jnp.int32, tile.shape, 1)
    cols = origin_ref[1] + lax.broadcasted_iota(jnp.int32, tile.shape, 2)
    out_ref[...] = jnp.where(jnp.maximum(rows, cols) < size, tile, jnp.zeros((), tile.dtype))


def masked_fronts(fronts, sizes, origin):
    local, rows, cols = fronts.shape
    step = 64
    spec = pl.BlockSpec((1, step, cols), lambda f, i: (f, i, 0))
    scalars = pl.BlockSpec(memory_space=pltpu.SMEM)
    return pl.pallas_call(
        mask_kernel,
        grid=(local, rows // step),
        in_specs=[scalars, scalars, spec],
        out_specs=spec,
        out_shape=jax.ShapeDtypeStruct(fronts.shape, fronts.dtype),
        compiler_params=pltpu.CompilerParams(vmem_limit_bytes=4 << 20),
    )(sizes, origin, fronts)


def reduce_core(partial, x, c):
    odd = (x - c) & 1
    received = shift(pick(partial, 1 - odd), "c", 1)
    total = pick(partial, odd).astype(F32) + received.astype(F32)
    return rolled(total, (((x - odd) & 3) >> 1,))


def first_pieces(product):
    block = product.shape[0] // 4
    half = block // 2
    to_right = product[block + half : 2 * block + half]
    to_left = jnp.concatenate([product[block : block + half], product[3 * block + half :]], axis=0)
    return to_right, to_left


def first_step(pieces):
    to_right, to_left = pieces
    return lax.optimization_barrier((shift(to_right, "x", 1), shift(to_left, "x", -1)))


def second_pieces(product, near):
    block = product.shape[0] // 4
    half = block // 2
    from_left, from_right = near
    over_right = product[2 * block + half : 3 * block].astype(F32) + from_left[:half].astype(F32)
    over_left = product[3 * block : 3 * block + half].astype(F32) + from_right[:half].astype(F32)
    return over_right.astype(BF16), over_left.astype(BF16)


def second_step(pieces):
    over_right, over_left = pieces
    return lax.optimization_barrier((shift(over_right, "x", 1), shift(over_left, "x", -1)))


def last_step(product, near, far):
    block = product.shape[0] // 4
    half = block // 2
    rows = block // 4
    (from_left, from_right), (over_right, over_left) = near, far
    top = product[:half].astype(F32) + from_left[half:].astype(F32) + over_left.astype(F32)
    low = product[half:block].astype(F32) + from_right[half:].astype(F32) + over_right.astype(F32)
    own = jnp.concatenate([top, low], axis=0)
    total = own[:rows]
    for k in (1, 2, 3):
        piece = own[k * rows : (k + 1) * rows].astype(BF16)
        total = total + shift(piece, "z", k).astype(F32)
    return total


def route_weight(parent_ids, block_maps, local):
    count, blocks = block_maps.shape
    order = (count // local, local, blocks)
    parent = jnp.broadcast_to(parent_ids[:, None], block_maps.shape).reshape(order)
    parent = parent.transpose(0, 2, 1).reshape(1, -1)
    block = block_maps.reshape(order).transpose(0, 2, 1).reshape(1, -1)
    index = lax.broadcasted_iota(jnp.int32, (count * blocks, 1), 0)
    to_parent = index // (blocks * local) * local + index % local
    to_block = index // local % blocks
    return ((parent == to_parent) & (block == to_block)).astype(BF16)


def shards(fronts, samples, second_samples, front_sizes, parent_ids, block_maps):
    local, tile_rows, tile_cols = fronts.shape
    own_rows = samples.shape[0]
    slab = second_samples.shape[0]
    group, x, z, h, c = (lax.axis_index(axis) for axis in DEVICES)
    row = lax.axis_index(ROW)
    col = lax.axis_index(COL)

    mine = jnp.stack([samples[:, f, :] for f in range(local)])
    columns = lax.all_gather(mine, "z", axis=1, tiled=True)
    gathered = gather_rows(columns)
    sizes = lax.dynamic_slice_in_dim(front_sizes, group * local, local, 0)
    second, sizes, columns = lax.optimization_barrier((second_samples, sizes, columns))
    second_of_pair = shift(second, "h", 1)
    masked = masked_fronts(fronts, sizes, jnp.stack([row * tile_rows, col * tile_cols]))
    weight = route_weight(parent_ids, block_maps, local)
    first = jnp.broadcast_to(h == 0, (1, tile_rows))
    gathered[0], second_of_pair, weight, first = lax.optimization_barrier(
        (gathered[0], second_of_pair, weight, first)
    )
    second = rolled(jnp.stack([second, second_of_pair]), (h,))

    halves = []
    for f in range(local):
        partial = jnp.einsum("sk,mk->sm", gathered[f], masked[f], preferred_element_type=F32)
        halves.append(reduce_core(partial.astype(BF16).reshape(2, 2, slab, tile_rows), x, c))

    spread = ("h", "group") + ROW
    outgoing = jnp.stack([half.astype(BF16).reshape(2 * slab, tile_rows) for half in halves], axis=1)
    arrived = lax.all_to_all(outgoing, spread, split_axis=0, concat_axis=0, tiled=True)
    arrived = arrived[:slab].astype(F32) + arrived[slab:].astype(F32)
    arrived = arrived.astype(BF16).reshape(-1, tile_rows)
    extension = jnp.einsum("ij,jk->ik", weight, arrived, preferred_element_type=F32).astype(BF16)
    extension = extension.reshape(slab, local, tile_rows)
    extension = jnp.concatenate([extension, extension], axis=0)
    extension = lax.all_to_all(extension, spread, split_axis=0, concat_axis=0, tiled=True)
    combined = second.reshape(extension.shape).astype(F32) + extension.astype(F32)
    combined = combined.astype(BF16)

    nearer = ((x + ((c - x) & 1)) & 3) >> 1
    ordered = []
    for f in range(local):
        mine = combined[:, f, :].reshape(2, -1, own_rows, tile_rows)
        ordered.append(rolled(mine, (nearer, z)).reshape(2 * slab, tile_rows))
    everyone = lax.all_gather(jnp.stack(ordered), "c", axis=0)
    ordered = [rolled(everyone[:, f], (x & 1,)).reshape(4 * slab, tile_rows) for f in range(local)]

    def multiplied(f):
        product = jnp.einsum("sm,mk->sk", ordered[f], masked[f], preferred_element_type=F32)
        return product.astype(BF16)

    product_0 = multiplied(0)
    product_0, *halves = lax.optimization_barrier((product_0, *halves))
    pieces_0 = first_pieces(product_0)
    near_0 = first_step(pieces_0)
    away = jnp.stack([jnp.where(first, half[1], half[0]).astype(BF16) for half in halves])
    away, _ = lax.optimization_barrier((away, pieces_0))
    received = shift(away, "h", 1)
    ordered[1], _ = lax.optimization_barrier((ordered[1], (pieces_0, away)))
    product_1 = multiplied(1)
    pieces_1 = first_pieces(product_1)
    near_0, product_1, pieces_1, received = lax.optimization_barrier((near_0, product_1, pieces_1, received))
    far_0 = second_step(second_pieces(product_0, near_0))
    near_1 = first_step(pieces_1)
    total_0 = last_step(product_0, near_0, far_0)
    passed_1 = second_pieces(product_1, near_1)
    far_1 = second_step(passed_1)
    received, _ = lax.optimization_barrier((received, far_1))
    slabs = [jnp.where(first, half[0], half[1]) + received[f].astype(F32) for f, half in enumerate(halves)]
    sampled = jnp.stack([total.astype(BF16) for total in slabs], axis=1)
    total_1 = last_step(product_1, near_1, far_1)
    outs = [total_0.astype(BF16), total_1.astype(BF16)]
    return sampled, jnp.stack(outs, axis=1)


def solution(mesh):
    torus = Mesh(mesh.devices.reshape(mesh.shape["group"], 4, 4, 2, 2), DEVICES)
    in_specs = (P("group", ROW, COL), P(ROW, "group", COL), P(COL, "group", ROW), P(), P(), P())
    out_specs = (P(COL, "group", ROW), P(ROW, "group", COL))
    return jax.shard_map(
        shards, mesh=torus, in_specs=in_specs, out_specs=out_specs, check_vma=False
    )
```
